32 devices in a mesh: dp: 4 (over y, x), ctx: 8 (over z, core).
Axes of the slice: x: 2, y: 2, z: 4, core: 2. Of those that a mesh axis runs over, the one named last changes fastest.
Arguments:
- layer_input: bfloat16 [4, 1024, 2048], P('dp', 'ctx'), may hold values from -6 to 6
- cotangent: bfloat16 [4, 1024, 2048], P('dp', 'ctx'), may hold values from -6 to 6
- prefix: int32 [4], P('dp'), may hold values from 102 to 512
- w_query: float32 [2048, 2048], P(('dp', 'ctx')), may hold values from -0.125 to 0.125
- key_weight: float32 [2048, 1024], P(('dp', 'ctx')), may hold values from -0.125 to 0.125
- value_weight: float32 [2048, 1024], P(('dp', 'ctx')), may hold values from -0.125 to 0.125
- w_out: float32 [2048, 2048], P(('dp', 'ctx')), may hold values from -1.25 to 1.25
- w_gate: float32 [2048, 8192], P(('dp', 'ctx')), may hold values from -0.125 to 0.125
- w_up: float32 [2048, 8192], P(('dp', 'ctx')), may hold values from -0.125 to 0.125
- w_down: float32 [8192, 2048], P(('dp', 'ctx')), may hold values from -0.0625 to 0.0625
- attention_norm_gain: float32 [2048], P(('dp', 'ctx')), may hold values from 0.5 to 1.5
- feedforward_norm_gain: float32 [2048], P(('dp', 'ctx')), may hold values from 0.5 to 1.5
Outputs:
- output: bfloat16 [4, 1024, 2048], P('dp', 'ctx')
- input_grad: bfloat16 [4, 1024, 2048], P('dp', 'ctx')
- w_query_grad: float32 [2048, 2048], P(('dp', 'ctx'))
- w_key_grad: float32 [2048, 1024], P(('dp', 'ctx'))
- w_value_grad: float32 [2048, 1024], P(('dp', 'ctx'))
- w_out_grad: float32 [2048, 2048], P(('dp', 'ctx'))
- w_gate_grad: float32 [2048, 8192], P(('dp', 'ctx'))
- w_up_grad: float32 [2048, 8192], P(('dp', 'ctx'))
- w_down_grad: float32 [8192, 2048], P(('dp', 'ctx'))
- gain_attn_grad: float32 [2048], P(('dp', 'ctx'))
- gain_mlp_grad: float32 [2048], P(('dp', 'ctx'))
The draws below stay inside these ranges and needn't reach their ends.
Inputs may be any that keep to these rules, and one draw needn't show every extreme that they name: `prefix`: the number of leading tokens of each sequence that attend to one another both ways.
All inputs are finite; a program needn't handle non-finite values.
Results may differ from the reference program's by a relative error of at most 0.025.
Values may be sent and summed in bfloat16 or wider, within the bound.
No kernel may reach another device: no remote copies, remote signals or barrier semaphores. Data moves between devices by JAX's collectives and lax.ppermute only.
A program may use at most 640 MiB of HBM per device.

```python
import jax
import jax.numpy as jnp
from jax import lax

MODEL_WIDTH = 2048
FF = 8192
QUERY_HEADS = 8
KEY_VALUE_HEADS = 4
HEAD_SIZE = 256
PIECE_TOKENS = 128
SEQ_LEN = 1024
SEQS = 4


def set_ends(array, stream_key, smallest, largest):
    shape = array.shape
    place = [jax.random.randint(jax.random.fold_in(stream_key, axis), (), 0, shape[axis]) for axis in range(len(shape))]
    array = array.at[tuple(place)].set(smallest)
    longest = shape.index(max(shape))
    place[longest] = (place[longest] + 1) % shape[longest]
    return array.at[tuple(place)].set(largest)


def block_levels(stream_key, dims, shards, low, largest):
    level = 1.0
    for dim, parts in shards:
        steps = jax.random.uniform(jax.random.fold_in(jax.random.fold_in(stream_key, 6), dim), (parts,), jnp.float32, low / len(shards), largest / len(shards))
        level = level * jnp.repeat(jnp.exp(steps), dims[dim] // parts).reshape((-1,) + (1,) * (len(dims) - 1 - dim))
    return level


def noise(stream_key, dims, scale, bound, shards=(), kind=jnp.bfloat16):
    values = jax.random.normal(stream_key, dims, jnp.float32) * scale
    if len(shards) > 0:
        values = block_levels(stream_key, dims, shards, -0.22, 0.18) * values
    return jnp.clip(values, min=-bound, max=bound).astype(kind)


def setup_inputs(seed: int = 0) -> dict:
    keys = jax.random.split(jax.random.key(seed), 13)
    layer_input = noise(keys[0], (SEQS, SEQ_LEN, MODEL_WIDTH), 1.0, 6.0, ((0, 4), (1, 8)))
    cotangent = noise(keys[1], (SEQS, SEQ_LEN, MODEL_WIDTH), 1.0, 6.0, ((0, 4), (1, 8)))
    prefix = set_ends(jax.random.randint(keys[2], (SEQS,), SEQ_LEN // 10, SEQ_LEN // 2 + 1), jax.random.fold_in(keys[2], 1), SEQ_LEN // 10, (SEQ_LEN // 2 + 1) - 1).astype(jnp.int32)
    w_query = noise(keys[3], (MODEL_WIDTH, QUERY_HEADS * HEAD_SIZE), MODEL_WIDTH ** -0.5, 0.125, ((0, 32),), jnp.float32)
    key_weight = noise(keys[4], (MODEL_WIDTH, KEY_VALUE_HEADS * HEAD_SIZE), MODEL_WIDTH ** -0.5, 0.125, ((0, 32),), jnp.float32)
    value_weight = noise(keys[5], (MODEL_WIDTH, KEY_VALUE_HEADS * HEAD_SIZE), MODEL_WIDTH ** -0.5, 0.125, ((0, 32),), jnp.float32)
    w_out = noise(keys[6], (QUERY_HEADS * HEAD_SIZE, MODEL_WIDTH), (max(1, QUERY_HEADS * HEAD_SIZE * 12 // SEQ_LEN)) ** -0.5, 1.25, ((0, 32),), jnp.float32)
    w_gate = noise(keys[7], (MODEL_WIDTH, FF), MODEL_WIDTH ** -0.5, 0.125, ((0, 32),), jnp.float32)
    w_up = noise(keys[8], (MODEL_WIDTH, FF), MODEL_WIDTH ** -0.5, 0.125, ((0, 32),), jnp.float32)
    w_down = noise(keys[9], (FF, MODEL_WIDTH), FF ** -0.5, 0.0625, ((0, 32),), jnp.float32)
    attention_norm_gain = jnp.clip(1.0 + 0.1 * jax.random.normal(keys[10], (MODEL_WIDTH,), jnp.float32), 0.5, 1.5)
    feedforward_norm_gain = jnp.clip(1.0 + 0.1 * jax.random.normal(keys[11], (MODEL_WIDTH,), jnp.float32), 0.5, 1.5)
    return {"layer_input": layer_input, "cotangent": cotangent, "prefix": prefix, "w_query": w_query, "key_weight": key_weight, "value_weight": value_weight, "w_out": w_out, "w_gate": w_gate, "w_up": w_up, "w_down": w_down, "attention_norm_gain": attention_norm_gain, "feedforward_norm_gain": feedforward_norm_gain}


NORM_EPSILON = 1e-06
THETA = 1000042.0

@jax.custom_vjp
def lowered_precision(v):
    return lax.optimization_barrier(v.astype(jnp.bfloat16)).astype(jnp.float32)

@jax.custom_vjp
def lowered_backward(v):
    return v

def low_keep(v):
    return (lowered_precision(v), None)

def low_pass(kept, grad):
    return (grad,)

def back_keep(v):
    return (v, None)

def back_low(kept, grad):
    return (lowered_precision(grad),)
lowered_precision.defvjp(low_keep, low_pass)
lowered_backward.defvjp(back_keep, back_low)

def rope_angles(token_positions, width):
    half_width = width // 2
    frequency = jnp.power(THETA, -(2.0 * jnp.arange(half_width, dtype=jnp.float32) / width))
    angles = token_positions.astype(jnp.float32)[:, None] * frequency[None, :]
    return (jnp.cos(angles)[:, None, :], jnp.sin(angles)[:, None, :])

def apply_rotary(vector, cosine_table, sines_lookup):
    half_width = vector.shape[-1] // 2
    first_half = vector[..., :half_width]
    second_half = vector[..., half_width:]
    return jnp.concatenate([first_half * cosine_table - second_half * sines_lookup, second_half * cosine_table + first_half * sines_lookup], axis=-1)

def layer(input_rows_all, w_query, key_weight, value_weight, w_out, w_gate, w_up, w_down, attention_norm_gain, feedforward_norm_gain, prefix_len):
    sequence_length = input_rows_all.shape[0]
    query_group_width = QUERY_HEADS // KEY_VALUE_HEADS
    attention_score_scale = HEAD_SIZE ** (-0.5)
    highest_accuracy = lax.Precision.HIGHEST
    token_positions = jnp.arange(sequence_length, dtype=jnp.int32)
    cosine_table, sines_lookup = rope_angles(token_positions, HEAD_SIZE)
    first_standardized = input_rows_all * lax.rsqrt(lax.optimization_barrier(jnp.mean(input_rows_all * input_rows_all, axis=-1, keepdims=True)) + NORM_EPSILON)
    first_normalized = lowered_precision(first_standardized * lowered_precision(attention_norm_gain))
    query_rows = lowered_backward(jnp.dot(first_normalized, lowered_precision(w_query), precision=highest_accuracy)).reshape(sequence_length, QUERY_HEADS, HEAD_SIZE)
    projected_keys = lowered_backward(jnp.dot(first_normalized, lowered_precision(key_weight), precision=highest_accuracy)).reshape(sequence_length, KEY_VALUE_HEADS, HEAD_SIZE)
    value_rows = lowered_precision(lowered_backward(jnp.dot(first_normalized, lowered_precision(value_weight), precision=highest_accuracy))).reshape(sequence_length, KEY_VALUE_HEADS, HEAD_SIZE)
    rotated_queries = lowered_precision(apply_rotary(query_rows, cosine_table, sines_lookup)).reshape(sequence_length, KEY_VALUE_HEADS, query_group_width, HEAD_SIZE)
    rotated_keys = lowered_precision(apply_rotary(projected_keys, cosine_table, sines_lookup))

    def apply_attention(block_item):
        query_block, row_block = block_item
        scores = jnp.einsum('bkgd,jkd->kgbj', query_block, rotated_keys, precision=highest_accuracy) * attention_score_scale
        scores = lowered_backward(scores)
        allowed = (token_positions[None, :] <= row_block[:, None]) | (token_positions[None, :] < prefix_len)
        scores = jnp.where(allowed[None, None], scores, -1e+30)
        row_maximum = lax.optimization_barrier(jnp.max(scores, axis=-1, keepdims=True))
        log_total = row_maximum + jnp.log(lax.optimization_barrier(jnp.sum(jnp.exp(scores - row_maximum), axis=-1, keepdims=True)))
        attn_probs = lowered_precision(jnp.exp(scores - log_total))
        return jnp.einsum('kgbj,jkd->bkgd', attn_probs, value_rows, precision=highest_accuracy)
    count_of_blocks = sequence_length // PIECE_TOKENS
    attention_result = lax.map(jax.checkpoint(apply_attention), (rotated_queries.reshape(count_of_blocks, PIECE_TOKENS, KEY_VALUE_HEADS, query_group_width, HEAD_SIZE), token_positions.reshape(count_of_blocks, PIECE_TOKENS)))
    attn_out = lowered_precision(lowered_backward(attention_result.reshape(sequence_length, QUERY_HEADS * HEAD_SIZE)))
    hidden_middle = input_rows_all + lowered_backward(jnp.dot(attn_out, lowered_precision(w_out), precision=highest_accuracy))
    second_standardized = hidden_middle * lax.rsqrt(lax.optimization_barrier(jnp.mean(hidden_middle * hidden_middle, axis=-1, keepdims=True)) + NORM_EPSILON)
    second_normalized = lowered_precision(second_standardized * lowered_precision(feedforward_norm_gain))
    gate_proj = lowered_backward(jnp.dot(second_normalized, lowered_precision(w_gate), precision=highest_accuracy))
    up_proj = lowered_backward(jnp.dot(second_normalized, lowered_precision(w_up), precision=highest_accuracy))
    hidden = lowered_precision(jax.nn.silu(gate_proj) * up_proj)
    return hidden_middle + lowered_backward(jnp.dot(hidden, lowered_precision(w_down), precision=highest_accuracy))

def reference(layer_input, cotangent, prefix, w_query, key_weight, value_weight, w_out, w_gate, w_up, w_down, attention_norm_gain, feedforward_norm_gain):
    weights = (w_query, key_weight, value_weight, w_out, w_gate, w_up, w_down, attention_norm_gain, feedforward_norm_gain)

    def per_sequence(totals, seq_item):
        input_seq, cot_seq, prefix_len = seq_item

        def forward(input_rows, *params):
            return layer(input_rows, *params, prefix_len)
        result, pullback = jax.vjp(forward, input_seq.astype(jnp.float32), *weights)
        gradients = pullback(cot_seq.astype(jnp.float32))
        totals = tuple((total_part + grad_part for total_part, grad_part in zip(totals, gradients[1:])))
        return (totals, (result.astype(jnp.bfloat16), gradients[0].astype(jnp.bfloat16)))
    zero_filled = tuple((jnp.zeros(weight.shape, jnp.float32) for weight in weights))
    totals, (output, input_grad) = lax.scan(per_sequence, zero_filled, (layer_input, cotangent, prefix))
    return (output, input_grad, totals[0], totals[1], totals[2], totals[3], totals[4], totals[5], totals[6], totals[7], totals[8])
```

```python
import jax
import jax.numpy as jnp
from jax import lax
from jax.sharding import PartitionSpec as P

FF = 8192
QUERY_HEADS = 8
KEY_VALUE_HEADS = 4
HEAD_SIZE = 256


NORM_EPSILON = 1e-06
THETA = 1000042.0


def rope_angles(token_positions, width):
    half_width = width // 2
    frequency = jnp.power(THETA, -(2.0 * jnp.arange(half_width, dtype=jnp.float32) / width))
    angles = token_positions.astype(jnp.float32)[:, None] * frequency[None, :]
    return (jnp.cos(angles)[:, None, :], jnp.sin(angles)[:, None, :])


def apply_rotary(vector, cosine_table, sines_lookup):
    half_width = vector.shape[-1] // 2
    first_half = vector[..., :half_width]
    second_half = vector[..., half_width:]
    return jnp.concatenate(
        [
            first_half * cosine_table - second_half * sines_lookup,
            second_half * cosine_table + first_half * sines_lookup,
        ],
        axis=-1,
    )


def reverse_rotary(vector, cosine_table, sines_lookup):
    half_width = vector.shape[-1] // 2
    first_half = vector[..., :half_width]
    second_half = vector[..., half_width:]
    return jnp.concatenate(
        [
            first_half * cosine_table + second_half * sines_lookup,
            second_half * cosine_table - first_half * sines_lookup,
        ],
        axis=-1,
    )


def norm_backward(d_normed, hat_values, gain_row, inverse):
    scaled = d_normed * gain_row
    return inverse * (scaled - hat_values * jnp.mean(scaled * hat_values, axis=-1, keepdims=True))


def column_product(left, right):
    return jnp.einsum("bd,bf->df", left, right, preferred_element_type=jnp.float32)


def gathered_local(
    layer_input,
    cotangent,
    prefix,
    w_query,
    key_weight,
    value_weight,
    w_out,
    w_gate,
    w_up,
    w_down,
    attention_norm_gain,
    feedforward_norm_gain,
):
    narrow_number_type = jnp.bfloat16
    wide_number_type = jnp.float32
    token_rows = layer_input.shape[1]
    query_group_width = QUERY_HEADS // KEY_VALUE_HEADS
    attention_score_scale = HEAD_SIZE ** (-0.5)
    input_rows_all = layer_input[0].astype(wide_number_type)
    first_row = lax.axis_index("ctx") * token_rows
    token_positions = first_row + jnp.arange(token_rows, dtype=jnp.int32)
    prefix_len = prefix[0]
    cosine_table, sines_lookup = rope_angles(token_positions, HEAD_SIZE)
    attn_kept = (
        lax.all_gather(w_query.astype(narrow_number_type), ("dp", "ctx"), axis=0, tiled=True),
        lax.all_gather(key_weight.astype(narrow_number_type), ("dp", "ctx"), axis=0, tiled=True),
        lax.all_gather(value_weight.astype(narrow_number_type), ("dp", "ctx"), axis=0, tiled=True),
        lax.all_gather(w_out.astype(narrow_number_type), ("dp", "ctx"), axis=0, tiled=True),
        lax.all_gather(
            attention_norm_gain.astype(narrow_number_type), ("dp", "ctx"), axis=0, tiled=True
        ),
    )
    query_w, key_matrix, value_w, out_w, attention_gain = attn_kept
    first_inverse_norm = lax.rsqrt(
        jnp.mean(input_rows_all * input_rows_all, axis=-1, keepdims=True) + NORM_EPSILON
    )
    first_standardized = input_rows_all * first_inverse_norm
    first_normalized = (first_standardized * attention_gain.astype(wide_number_type)).astype(
        narrow_number_type
    )
    query_rows = jnp.dot(
        first_normalized, query_w, preferred_element_type=wide_number_type
    ).reshape(token_rows, QUERY_HEADS, HEAD_SIZE)
    projected_keys = jnp.dot(
        first_normalized, key_matrix, preferred_element_type=wide_number_type
    ).reshape(token_rows, KEY_VALUE_HEADS, HEAD_SIZE)
    value_rows = jnp.dot(first_normalized, value_w, preferred_element_type=wide_number_type).astype(
        narrow_number_type
    )
    rotated_queries = apply_rotary(query_rows, cosine_table, sines_lookup).astype(
        narrow_number_type
    )
    rotated_keys = (
        apply_rotary(projected_keys, cosine_table, sines_lookup)
        .astype(narrow_number_type)
        .reshape(token_rows, KEY_VALUE_HEADS * HEAD_SIZE)
    )
    grouped_queries = rotated_queries.reshape(
        token_rows, KEY_VALUE_HEADS, query_group_width, HEAD_SIZE
    )

    def masked_scores(key_segment, start_row):
        segment_rows = key_segment.shape[0]
        columns = start_row + jnp.arange(segment_rows, dtype=jnp.int32)
        allowed = (columns[None, :] <= token_positions[:, None]) | (columns[None, :] < prefix_len)
        scores = (
            jnp.einsum(
                "bkgd,jkd->kgbj",
                grouped_queries,
                key_segment.reshape(segment_rows, KEY_VALUE_HEADS, HEAD_SIZE),
                preferred_element_type=wide_number_type,
            )
            * attention_score_scale
        )
        return jnp.where(allowed[None, None], scores, -jnp.inf)

    row_maximum = jnp.full(
        (KEY_VALUE_HEADS, query_group_width, token_rows), -1e30, wide_number_type
    )
    key_segment = lax.all_gather(rotated_keys, "ctx", axis=0, tiled=True)
    value_segment = lax.all_gather(value_rows, "ctx", axis=0, tiled=True)
    segment_rows = value_segment.shape[0]
    scores = masked_scores(key_segment, jnp.int32(0))
    new_peak = jnp.maximum(row_maximum, jnp.max(scores, axis=-1))
    soft_part = jnp.exp(scores - new_peak[..., None])
    row_denominator = jnp.sum(soft_part, axis=-1)
    weighted_values = jnp.einsum(
        "kgbj,jkd->bkgd",
        soft_part.astype(narrow_number_type),
        value_segment.reshape(segment_rows, KEY_VALUE_HEADS, HEAD_SIZE),
        preferred_element_type=wide_number_type,
    )
    row_maximum, row_denominator, weighted_values = (new_peak, row_denominator, weighted_values)
    log_total = row_maximum + jnp.log(row_denominator)
    attention_result = weighted_values / jnp.transpose(row_denominator, (2, 0, 1))[..., None]
    attn_out = attention_result.reshape(token_rows, QUERY_HEADS * HEAD_SIZE).astype(
        narrow_number_type
    )
    hidden_middle = input_rows_all + jnp.dot(
        attn_out, out_w, preferred_element_type=wide_number_type
    )
    mlp_kept = (
        lax.all_gather(w_gate.astype(narrow_number_type), ("dp", "ctx"), axis=0, tiled=True),
        lax.all_gather(w_up.astype(narrow_number_type), ("dp", "ctx"), axis=0, tiled=True),
        lax.all_gather(w_down.astype(narrow_number_type), ("dp", "ctx"), axis=0, tiled=True),
        lax.all_gather(
            feedforward_norm_gain.astype(narrow_number_type), ("dp", "ctx"), axis=0, tiled=True
        ),
    )
    gate_w, up_w, down_w, feedforward_gain = mlp_kept
    second_inverse_norm = lax.rsqrt(
        jnp.mean(hidden_middle * hidden_middle, axis=-1, keepdims=True) + NORM_EPSILON
    )
    second_standardized = hidden_middle * second_inverse_norm
    second_normalized = (second_standardized * feedforward_gain.astype(wide_number_type)).astype(
        narrow_number_type
    )
    gate_proj = jnp.dot(second_normalized, gate_w, preferred_element_type=wide_number_type)
    up_proj = jnp.dot(second_normalized, up_w, preferred_element_type=wide_number_type)
    hidden = (jax.nn.silu(gate_proj) * up_proj).astype(narrow_number_type)
    result = hidden_middle + jnp.dot(hidden, down_w, preferred_element_type=wide_number_type)
    output = result.astype(narrow_number_type)[None]
    gate_w, up_w, down_w, feedforward_gain = (
        lax.all_gather(w_gate.astype(narrow_number_type), ("dp", "ctx"), axis=0, tiled=True),
        lax.all_gather(w_up.astype(narrow_number_type), ("dp", "ctx"), axis=0, tiled=True),
        lax.all_gather(w_down.astype(narrow_number_type), ("dp", "ctx"), axis=0, tiled=True),
        lax.all_gather(
            feedforward_norm_gain.astype(narrow_number_type), ("dp", "ctx"), axis=0, tiled=True
        ),
    )
    d_out = cotangent[0]
    down_sum = lax.psum_scatter(
        column_product(hidden, d_out), ("dp", "ctx"), scatter_dimension=0, tiled=True
    )
    d_hidden = jnp.einsum("bd,fd->bf", d_out, down_w, preferred_element_type=wide_number_type)
    sigmoid_gate = jax.nn.sigmoid(gate_proj)
    d_gate = (d_hidden * up_proj * sigmoid_gate * (1.0 + gate_proj * (1.0 - sigmoid_gate))).astype(
        narrow_number_type
    )
    d_up = (d_hidden * gate_proj * sigmoid_gate).astype(narrow_number_type)
    second_normalized_gradient = jnp.einsum(
        "bf,df->bd", d_gate, gate_w, preferred_element_type=wide_number_type
    ) + jnp.einsum("bf,df->bd", d_up, up_w, preferred_element_type=wide_number_type)
    gate_and_up = jnp.concatenate([d_gate, d_up], axis=1)
    both_sum = lax.psum_scatter(
        column_product(second_normalized, gate_and_up),
        ("dp", "ctx"),
        scatter_dimension=0,
        tiled=True,
    )
    gate_sum = both_sum[:, :FF]
    up_sum = both_sum[:, FF:]
    feedforward_gain_part = jnp.sum(second_normalized_gradient * second_standardized, axis=0)
    middle_gradient = d_out.astype(wide_number_type) + norm_backward(
        second_normalized_gradient,
        second_standardized,
        feedforward_gain.astype(wide_number_type),
        second_inverse_norm,
    )
    query_w, key_matrix, value_w, out_w, attention_gain = (
        lax.all_gather(w_query.astype(narrow_number_type), ("dp", "ctx"), axis=0, tiled=True),
        lax.all_gather(key_weight.astype(narrow_number_type), ("dp", "ctx"), axis=0, tiled=True),
        lax.all_gather(value_weight.astype(narrow_number_type), ("dp", "ctx"), axis=0, tiled=True),
        lax.all_gather(w_out.astype(narrow_number_type), ("dp", "ctx"), axis=0, tiled=True),
        lax.all_gather(
            attention_norm_gain.astype(narrow_number_type), ("dp", "ctx"), axis=0, tiled=True
        ),
    )
    d_branch = middle_gradient.astype(narrow_number_type)
    out_sum = lax.psum_scatter(
        column_product(attn_out, d_branch), ("dp", "ctx"), scatter_dimension=0, tiled=True
    )
    attention_gradient = jnp.einsum(
        "bd,hd->bh", d_branch, out_w, preferred_element_type=wide_number_type
    ).astype(narrow_number_type)
    attention_group_gradient = attention_gradient.reshape(
        token_rows, KEY_VALUE_HEADS, query_group_width, HEAD_SIZE
    )
    delta_rows = jnp.transpose(
        jnp.sum(attention_group_gradient.astype(wide_number_type) * attention_result, axis=-1),
        (1, 2, 0),
    )
    gathered_keys, gathered_values = (
        lax.all_gather(rotated_keys, "ctx", axis=0, tiled=True),
        lax.all_gather(value_rows, "ctx", axis=0, tiled=True),
    )
    count_of_blocks = gathered_keys.shape[0] // token_rows
    stacked_key_blocks = gathered_keys.reshape(
        count_of_blocks, token_rows, KEY_VALUE_HEADS * HEAD_SIZE
    )
    stacked_value_blocks = gathered_values.reshape(
        count_of_blocks, token_rows, KEY_VALUE_HEADS, HEAD_SIZE
    )

    def back_step(d_query_sum, block_item):
        current_key_block, value_block, block_index = block_item
        scores = masked_scores(current_key_block, block_index * token_rows)
        soft_part = jnp.exp(scores - log_total[..., None])
        d_value_block = jnp.einsum(
            "kgbj,bkgd->jkd",
            soft_part.astype(narrow_number_type),
            attention_group_gradient,
            preferred_element_type=wide_number_type,
        )
        d_probs = jnp.einsum(
            "bkgd,jkd->kgbj",
            attention_group_gradient,
            value_block,
            preferred_element_type=wide_number_type,
        )
        d_scores = (soft_part * (d_probs - delta_rows[..., None])).astype(narrow_number_type)
        key_tensor_triple = current_key_block.reshape(token_rows, KEY_VALUE_HEADS, HEAD_SIZE)
        d_query_sum = d_query_sum + jnp.einsum(
            "kgbj,jkd->bkgd", d_scores, key_tensor_triple, preferred_element_type=wide_number_type
        )
        d_key_block = jnp.einsum(
            "kgbj,bkgd->jkd", d_scores, grouped_queries, preferred_element_type=wide_number_type
        )
        return (d_query_sum, (d_key_block, d_value_block))

    d_query_sum, (key_gradients, value_gradients) = lax.scan(
        back_step,
        jnp.zeros((token_rows, KEY_VALUE_HEADS, query_group_width, HEAD_SIZE), wide_number_type),
        (stacked_key_blocks, stacked_value_blocks, jnp.arange(count_of_blocks, dtype=jnp.int32)),
    )
    key_gradients = (
        key_gradients.reshape(count_of_blocks * token_rows, KEY_VALUE_HEADS * HEAD_SIZE)
        * attention_score_scale
    )
    value_gradients = value_gradients.reshape(
        count_of_blocks * token_rows, KEY_VALUE_HEADS * HEAD_SIZE
    )
    local_keys, own_values = (
        lax.psum_scatter(
            key_gradients.astype(jnp.bfloat16), "ctx", scatter_dimension=0, tiled=True
        ).astype(jnp.float32),
        lax.psum_scatter(
            value_gradients.astype(jnp.bfloat16), "ctx", scatter_dimension=0, tiled=True
        ).astype(jnp.float32),
    )
    d_key = (
        reverse_rotary(
            local_keys.reshape(token_rows, KEY_VALUE_HEADS, HEAD_SIZE), cosine_table, sines_lookup
        )
        .reshape(token_rows, KEY_VALUE_HEADS * HEAD_SIZE)
        .astype(narrow_number_type)
    )
    d_value = own_values.astype(narrow_number_type)
    d_query = reverse_rotary(
        (d_query_sum * attention_score_scale).reshape(token_rows, QUERY_HEADS, HEAD_SIZE),
        cosine_table,
        sines_lookup,
    )
    d_query = d_query.reshape(token_rows, QUERY_HEADS * HEAD_SIZE).astype(narrow_number_type)
    d_projected = jnp.concatenate([d_query, d_key, d_value], axis=1)
    projection_total = lax.psum_scatter(
        column_product(first_normalized, d_projected),
        ("dp", "ctx"),
        scatter_dimension=0,
        tiled=True,
    )
    query_sum = projection_total[:, : QUERY_HEADS * HEAD_SIZE]
    key_gradient_sum = projection_total[
        :, QUERY_HEADS * HEAD_SIZE : QUERY_HEADS * HEAD_SIZE + KEY_VALUE_HEADS * HEAD_SIZE
    ]
    value_gradient_sum = projection_total[
        :, QUERY_HEADS * HEAD_SIZE + KEY_VALUE_HEADS * HEAD_SIZE :
    ]
    first_normalized_gradient = (
        jnp.einsum("bh,dh->bd", d_query, query_w, preferred_element_type=wide_number_type)
        + jnp.einsum("bh,dh->bd", d_key, key_matrix, preferred_element_type=wide_number_type)
        + jnp.einsum("bh,dh->bd", d_value, value_w, preferred_element_type=wide_number_type)
    )
    attention_gain_part = jnp.sum(first_normalized_gradient * first_standardized, axis=0)
    gradient_of_input = middle_gradient + norm_backward(
        first_normalized_gradient,
        first_standardized,
        attention_gain.astype(wide_number_type),
        first_inverse_norm,
    )
    attn_gain_sum, mlp_gain_sum = (
        lax.psum_scatter(attention_gain_part, ("dp", "ctx"), scatter_dimension=0, tiled=True),
        lax.psum_scatter(feedforward_gain_part, ("dp", "ctx"), scatter_dimension=0, tiled=True),
    )
    input_grad = gradient_of_input.astype(narrow_number_type)[None]
    return (
        output,
        input_grad,
        query_sum,
        key_gradient_sum,
        value_gradient_sum,
        out_sum,
        gate_sum,
        up_sum,
        down_sum,
        attn_gain_sum,
        mlp_gain_sum,
    )

def swap_cores(values):
    size = lax.axis_size("ctx")
    return lax.ppermute(values, "ctx", [(i, i ^ 1) for i in range(size)])


def gather_ctx(rows):
    return lax.all_gather(rows, "ctx", axis=0, tiled=True)


def scatter_ctx(partial):
    return lax.psum_scatter(partial, "ctx", scatter_dimension=0, tiled=True).astype(jnp.float32)


def gather_dp(rows):
    return lax.all_gather(rows, "dp", axis=0, tiled=True)


def scatter_dp(partial):
    return lax.psum_scatter(partial, "dp", scatter_dimension=0, tiled=True)


def exchange_ctx(blocks):
    return lax.all_to_all(blocks, "ctx", 0, 0, tiled=True)


def out_weight_moves(n_dp, n_ctx):
    per_head = n_dp * n_ctx // QUERY_HEADS
    moves = []
    for block in range(n_dp * n_ctx):
        head, part = divmod(block, per_head)
        moves.append((block, part * n_ctx + head))
    return moves


def head_local(
    layer_input,
    cotangent,
    prefix,
    w_query,
    key_weight,
    value_weight,
    w_out,
    w_gate,
    w_up,
    w_down,
    attention_norm_gain,
    feedforward_norm_gain,
):
    low = jnp.bfloat16
    wide = jnp.float32
    n_dp = lax.axis_size("dp")
    n_ctx = lax.axis_size("ctx")
    core = lax.axis_index("ctx") % 2
    rows = w_query.shape[0]
    seq_rows = layer_input.shape[1] * n_ctx
    ff_part = w_down.shape[0]

    def dot(left, right):
        return jnp.dot(left, right, preferred_element_type=wide)

    def dot_t(left, right):
        return lax.dot_general(left, right, (((1,), (1,)), ((), ())), preferred_element_type=wide)

    def t_dot(left, right):
        return lax.dot_general(left, right, (((0,), (0,)), ((), ())), preferred_element_type=wide)

    def lowered(weight):
        return weight.astype(low).astype(wide)

    x_rows = layer_input[0].astype(wide)
    d_out = cotangent[0]
    gain_a = lowered(attention_norm_gain)[:, None]
    gain_m = lowered(feedforward_norm_gain)[:, None]
    low_q, low_k, low_v = lowered(w_query), lowered(key_weight), lowered(value_weight)
    low_g, low_u = lowered(w_gate), lowered(w_up)

    inverse1 = lax.rsqrt(jnp.mean(x_rows * x_rows, axis=-1, keepdims=True) + NORM_EPSILON)
    hat1 = x_rows * inverse1
    all_hat1 = gather_ctx(hat1.astype(low))

    q_cols = (low_q * gain_a).astype(low).reshape(rows, n_ctx, 1, HEAD_SIZE)
    k_cols = (low_k * gain_a).astype(low).reshape(rows, n_ctx // 2, 1, 1, HEAD_SIZE)
    v_cols = (low_v * gain_a).astype(low).reshape(rows, n_ctx // 2, 1, 1, HEAD_SIZE)
    kv_cols = jnp.concatenate([k_cols, v_cols], axis=2).reshape(rows, n_ctx, 1, HEAD_SIZE)
    proj = jnp.concatenate([q_cols, kv_cols], axis=2).reshape(rows, n_ctx, 2 * HEAD_SIZE)
    proj = exchange_ctx(proj.transpose(1, 0, 2)).reshape(n_ctx * rows, 2 * HEAD_SIZE)
    proj = gather_dp(proj)
    moves = out_weight_moves(n_dp, n_ctx)
    out_w = gather_dp(lax.ppermute(w_out.astype(low), ("dp", "ctx"), moves))

    def ff_columns(weight):
        blocks = (weight * gain_m).astype(low).reshape(rows, n_dp, n_ctx, ff_part)
        return blocks.transpose(2, 0, 1, 3).reshape(n_ctx, rows, n_dp * ff_part)

    gate_up = jnp.concatenate([ff_columns(low_g), ff_columns(low_u)], axis=2)
    gate_up = exchange_ctx(gate_up).reshape(n_ctx * rows, 2 * n_dp * ff_part)
    gate_up_w = gather_dp(gate_up)
    down_w = gather_dp(w_down.astype(low))
    all_cot = gather_ctx(d_out)

    positions = jnp.arange(seq_rows, dtype=jnp.int32)
    cosine, sine = rope_angles(positions, HEAD_SIZE)
    cosine, sine = cosine[:, 0], sine[:, 0]
    half = HEAD_SIZE // 2

    def rotate(v, turn):
        a, b = v[:, :half], v[:, half:]
        return jnp.concatenate([a * cosine - turn * b * sine, b * cosine + turn * a * sine], axis=1)

    qkv = dot(all_hat1, proj)
    scale = HEAD_SIZE ** (-0.5)
    q_rot = (rotate(qkv[:, :HEAD_SIZE], 1.0) * scale).astype(low)
    own = qkv[:, HEAD_SIZE:]
    own = jnp.where(core == 0, rotate(own, 1.0), own).astype(low)
    other = swap_cores(own)
    keys = jnp.where(core == 0, own, other)
    values = jnp.where(core == 0, other, own)
    allowed = (positions[None, :] <= positions[:, None]) | (positions[None, :] < prefix[0])
    scores = jnp.where(allowed, dot_t(q_rot, keys), -1e30)
    peak = jnp.max(scores, axis=-1, keepdims=True)
    weights = jnp.exp(scores - peak)
    total = jnp.sum(weights, axis=-1, keepdims=True)
    attended = dot(weights.astype(low), values) / total
    attn = attended.astype(low)
    middle = x_rows + scatter_ctx(dot(attn, out_w).astype(low))

    inverse2 = lax.rsqrt(jnp.mean(middle * middle, axis=-1, keepdims=True) + NORM_EPSILON)
    hat2 = middle * inverse2
    all_hat2 = gather_ctx(hat2.astype(low))
    width = n_dp * ff_part
    gate = dot(all_hat2, gate_up_w[:, :width])
    up = dot(all_hat2, gate_up_w[:, width:])
    sig = jax.nn.sigmoid(gate)
    silu = gate * sig
    hidden = (silu * up).astype(low)
    output = (middle + scatter_ctx(dot(hidden, down_w).astype(low))).astype(low)[None]

    d_hidden = dot_t(all_cot, down_w)
    d_gate = (d_hidden * up * sig * (1.0 + gate * (1.0 - sig))).astype(low)
    d_up = (d_hidden * silu).astype(low)
    d_gate_up = jnp.concatenate([d_gate, d_up], axis=1)
    e2 = scatter_ctx(dot_t(d_gate_up, gate_up_w).astype(low))
    down_sum = scatter_dp(t_dot(hidden, all_cot).astype(low)).astype(wide)
    gate_up_sum = scatter_dp(t_dot(all_hat2, d_gate_up).astype(low))
    gate_up_sum = exchange_ctx(gate_up_sum.reshape(n_ctx, rows, 2 * width)).astype(wide)

    def ff_rows(part):
        blocks = part.reshape(n_ctx, rows, n_dp, ff_part).transpose(1, 2, 0, 3)
        return blocks.reshape(rows, n_dp * n_ctx * ff_part)

    raw_gate = ff_rows(gate_up_sum[:, :, :width])
    raw_up = ff_rows(gate_up_sum[:, :, width:])
    gain_mlp = jnp.sum(raw_gate * low_g, axis=1) + jnp.sum(raw_up * low_u, axis=1)
    gate_sum, up_sum = raw_gate * gain_m, raw_up * gain_m
    d_middle = d_out.astype(wide) + inverse2 * (
        e2 - hat2 * jnp.mean(e2 * hat2, axis=-1, keepdims=True)
    )

    all_branch = gather_ctx(d_middle.astype(low))
    out_sum = scatter_dp(t_dot(attn, all_branch).astype(low))
    out_sum = lax.ppermute(out_sum, ("dp", "ctx"), [(b, a) for a, b in moves]).astype(wide)
    d_attn = dot_t(all_branch, out_w).astype(low)
    delta = jnp.sum(d_attn.astype(wide) * attended, axis=-1, keepdims=True)
    probs = weights / total
    d_scores = (probs * (dot_t(d_attn, values) - delta)).astype(low)
    d_query = rotate(dot(d_scores, keys) * scale, -1.0)
    dk_part = t_dot(d_scores, q_rot)
    dv_part = t_dot(probs.astype(low), d_attn)
    mine = jnp.where(core == 0, dk_part, dv_part)
    mine = mine + swap_cores(jnp.where(core == 0, dv_part, dk_part).astype(low)).astype(wide)
    mine = jnp.where(core == 0, rotate(mine, -1.0), mine)
    d_proj = jnp.concatenate([d_query, mine], axis=1).astype(low)
    e1 = scatter_ctx(dot_t(d_proj, proj).astype(low))
    proj_sum = scatter_dp(t_dot(all_hat1, d_proj).astype(low))
    proj_sum = exchange_ctx(proj_sum.reshape(n_ctx, rows, 2 * HEAD_SIZE)).astype(wide)
    proj_sum = proj_sum.transpose(1, 0, 2)
    raw_q = proj_sum[:, :, :HEAD_SIZE].reshape(rows, n_ctx * HEAD_SIZE)
    kv_sum = proj_sum[:, :, HEAD_SIZE:].reshape(rows, n_ctx // 2, 2, HEAD_SIZE)
    raw_k = kv_sum[:, :, 0].reshape(rows, n_ctx // 2 * HEAD_SIZE)
    raw_v = kv_sum[:, :, 1].reshape(rows, n_ctx // 2 * HEAD_SIZE)
    gain_attn = (
        jnp.sum(raw_q * low_q, axis=1)
        + jnp.sum(raw_k * low_k, axis=1)
        + jnp.sum(raw_v * low_v, axis=1)
    )
    d_input = d_middle + inverse1 * (e1 - hat1 * jnp.mean(e1 * hat1, axis=-1, keepdims=True))
    return (
        output,
        d_input.astype(low)[None],
        raw_q * gain_a,
        raw_k * gain_a,
        raw_v * gain_a,
        out_sum,
        gate_sum,
        up_sum,
        down_sum,
        gain_attn,
        gain_mlp,
    )


def solution(mesh):
    local = head_local if mesh.shape["ctx"] == QUERY_HEADS else gathered_local
    in_specs = (
        P("dp", "ctx", None),
        P("dp", "ctx", None),
        P("dp"),
        P(("dp", "ctx"), None),
        P(("dp", "ctx"), None),
        P(("dp", "ctx"), None),
        P(("dp", "ctx"), None),
        P(("dp", "ctx"), None),
        P(("dp", "ctx"), None),
        P(("dp", "ctx"), None),
        P(("dp", "ctx")),
        P(("dp", "ctx")),
    )
    out_specs = (
        P("dp", "ctx", None),
        P("dp", "ctx", None),
        P(("dp", "ctx"), None),
        P(("dp", "ctx"), None),
        P(("dp", "ctx"), None),
        P(("dp", "ctx"), None),
        P(("dp", "ctx"), None),
        P(("dp", "ctx"), None),
        P(("dp", "ctx"), None),
        P(("dp", "ctx")),
        P(("dp", "ctx")),
    )
    return jax.shard_map(local, mesh=mesh, in_specs=in_specs, out_specs=out_specs, check_vma=False)
```

```python
import jax
import jax.numpy as jnp
from jax import lax
from jax.sharding import PartitionSpec as P

FF = 8192
QUERY_HEADS = 8
KEY_VALUE_HEADS = 4
HEAD_SIZE = 256


NORM_EPSILON = 1e-06
THETA = 1000042.0


def rope_angles(token_positions, width):
    half_width = width // 2
    frequency = jnp.power(THETA, -(2.0 * jnp.arange(half_width, dtype=jnp.float32) / width))
    angles = token_positions.astype(jnp.float32)[:, None] * frequency[None, :]
    return (jnp.cos(angles)[:, None, :], jnp.sin(angles)[:, None, :])


def apply_rotary(vector, cosine_table, sines_lookup):
    half_width = vector.shape[-1] // 2
    first_half = vector[..., :half_width]
    second_half = vector[..., half_width:]
    return jnp.concatenate(
        [
            first_half * cosine_table - second_half * sines_lookup,
            second_half * cosine_table + first_half * sines_lookup,
        ],
        axis=-1,
    )


def reverse_rotary(vector, cosine_table, sines_lookup):
    half_width = vector.shape[-1] // 2
    first_half = vector[..., :half_width]
    second_half = vector[..., half_width:]
    return jnp.concatenate(
        [
            first_half * cosine_table + second_half * sines_lookup,
            second_half * cosine_table - first_half * sines_lookup,
        ],
        axis=-1,
    )


def norm_backward(d_normed, hat_values, gain_row, inverse):
    scaled = d_normed * gain_row
    return inverse * (scaled - hat_values * jnp.mean(scaled * hat_values, axis=-1, keepdims=True))


def column_product(left, right):
    return jnp.einsum("bd,bf->df", left, right, preferred_element_type=jnp.float32)


def gathered_local(
    layer_input,
    cotangent,
    prefix,
    w_query,
    key_weight,
    value_weight,
    w_out,
    w_gate,
    w_up,
    w_down,
    attention_norm_gain,
    feedforward_norm_gain,
):
    narrow_number_type = jnp.bfloat16
    wide_number_type = jnp.float32
    token_rows = layer_input.shape[1]
    query_group_width = QUERY_HEADS // KEY_VALUE_HEADS
    attention_score_scale = HEAD_SIZE ** (-0.5)
    input_rows_all = layer_input[0].astype(wide_number_type)
    first_row = lax.axis_index("ctx") * token_rows
    token_positions = first_row + jnp.arange(token_rows, dtype=jnp.int32)
    prefix_len = prefix[0]
    cosine_table, sines_lookup = rope_angles(token_positions, HEAD_SIZE)
    attn_kept = (
        lax.all_gather(w_query.astype(narrow_number_type), ("dp", "ctx"), axis=0, tiled=True),
        lax.all_gather(key_weight.astype(narrow_number_type), ("dp", "ctx"), axis=0, tiled=True),
        lax.all_gather(value_weight.astype(narrow_number_type), ("dp", "ctx"), axis=0, tiled=True),
        lax.all_gather(w_out.astype(narrow_number_type), ("dp", "ctx"), axis=0, tiled=True),
        lax.all_gather(
            attention_norm_gain.astype(narrow_number_type), ("dp", "ctx"), axis=0, tiled=True
        ),
    )
    query_w, key_matrix, value_w, out_w, attention_gain = attn_kept
    first_inverse_norm = lax.rsqrt(
        jnp.mean(input_rows_all * input_rows_all, axis=-1, keepdims=True) + NORM_EPSILON
    )
    first_standardized = input_rows_all * first_inverse_norm
    first_normalized = (first_standardized * attention_gain.astype(wide_number_type)).astype(
        narrow_number_type
    )
    query_rows = jnp.dot(
        first_normalized, query_w, preferred_element_type=wide_number_type
    ).reshape(token_rows, QUERY_HEADS, HEAD_SIZE)
    projected_keys = jnp.dot(
        first_normalized, key_matrix, preferred_element_type=wide_number_type
    ).reshape(token_rows, KEY_VALUE_HEADS, HEAD_SIZE)
    value_rows = jnp.dot(first_normalized, value_w, preferred_element_type=wide_number_type).astype(
        narrow_number_type
    )
    rotated_queries = apply_rotary(query_rows, cosine_table, sines_lookup).astype(
        narrow_number_type
    )
    rotated_keys = (
        apply_rotary(projected_keys, cosine_table, sines_lookup)
        .astype(narrow_number_type)
        .reshape(token_rows, KEY_VALUE_HEADS * HEAD_SIZE)
    )
    grouped_queries = rotated_queries.reshape(
        token_rows, KEY_VALUE_HEADS, query_group_width, HEAD_SIZE
    )

    def masked_scores(key_segment, start_row):
        segment_rows = key_segment.shape[0]
        columns = start_row + jnp.arange(segment_rows, dtype=jnp.int32)
        allowed = (columns[None, :] <= token_positions[:, None]) | (columns[None, :] < prefix_len)
        scores = (
            jnp.einsum(
                "bkgd,jkd->kgbj",
                grouped_queries,
                key_segment.reshape(segment_rows, KEY_VALUE_HEADS, HEAD_SIZE),
                preferred_element_type=wide_number_type,
            )
            * attention_score_scale
        )
        return jnp.where(allowed[None, None], scores, -jnp.inf)

    row_maximum = jnp.full(
        (KEY_VALUE_HEADS, query_group_width, token_rows), -1e30, wide_number_type
    )
    key_segment = lax.all_gather(rotated_keys, "ctx", axis=0, tiled=True)
    value_segment = lax.all_gather(value_rows, "ctx", axis=0, tiled=True)
    segment_rows = value_segment.shape[0]
    scores = masked_scores(key_segment, jnp.int32(0))
    new_peak = jnp.maximum(row_maximum, jnp.max(scores, axis=-1))
    soft_part = jnp.exp(scores - new_peak[..., None])
    row_denominator = jnp.sum(soft_part, axis=-1)
    weighted_values = jnp.einsum(
        "kgbj,jkd->bkgd",
        soft_part.astype(narrow_number_type),
        value_segment.reshape(segment_rows, KEY_VALUE_HEADS, HEAD_SIZE),
        preferred_element_type=wide_number_type,
    )
    row_maximum, row_denominator, weighted_values = (new_peak, row_denominator, weighted_values)
    log_total = row_maximum + jnp.log(row_denominator)
    attention_result = weighted_values / jnp.transpose(row_denominator, (2, 0, 1))[..., None]
    attn_out = attention_result.reshape(token_rows, QUERY_HEADS * HEAD_SIZE).astype(
        narrow_number_type
    )
    hidden_middle = input_rows_all + jnp.dot(
        attn_out, out_w, preferred_element_type=wide_number_type
    )
    mlp_kept = (
        lax.all_gather(w_gate.astype(narrow_number_type), ("dp", "ctx"), axis=0, tiled=True),
        lax.all_gather(w_up.astype(narrow_number_type), ("dp", "ctx"), axis=0, tiled=True),
        lax.all_gather(w_down.astype(narrow_number_type), ("dp", "ctx"), axis=0, tiled=True),
        lax.all_gather(
            feedforward_norm_gain.astype(narrow_number_type), ("dp", "ctx"), axis=0, tiled=True
        ),
    )
    gate_w, up_w, down_w, feedforward_gain = mlp_kept
    second_inverse_norm = lax.rsqrt(
        jnp.mean(hidden_middle * hidden_middle, axis=-1, keepdims=True) + NORM_EPSILON
    )
    second_standardized = hidden_middle * second_inverse_norm
    second_normalized = (second_standardized * feedforward_gain.astype(wide_number_type)).astype(
        narrow_number_type
    )
    gate_proj = jnp.dot(second_normalized, gate_w, preferred_element_type=wide_number_type)
    up_proj = jnp.dot(second_normalized, up_w, preferred_element_type=wide_number_type)
    hidden = (jax.nn.silu(gate_proj) * up_proj).astype(narrow_number_type)
    result = hidden_middle + jnp.dot(hidden, down_w, preferred_element_type=wide_number_type)
    output = result.astype(narrow_number_type)[None]
    gate_w, up_w, down_w, feedforward_gain = (
        lax.all_gather(w_gate.astype(narrow_number_type), ("dp", "ctx"), axis=0, tiled=True),
        lax.all_gather(w_up.astype(narrow_number_type), ("dp", "ctx"), axis=0, tiled=True),
        lax.all_gather(w_down.astype(narrow_number_type), ("dp", "ctx"), axis=0, tiled=True),
        lax.all_gather(
            feedforward_norm_gain.astype(narrow_number_type), ("dp", "ctx"), axis=0, tiled=True
        ),
    )
    d_out = cotangent[0]
    down_sum = lax.psum_scatter(
        column_product(hidden, d_out), ("dp", "ctx"), scatter_dimension=0, tiled=True
    )
    d_hidden = jnp.einsum("bd,fd->bf", d_out, down_w, preferred_element_type=wide_number_type)
    sigmoid_gate = jax.nn.sigmoid(gate_proj)
    d_gate = (d_hidden * up_proj * sigmoid_gate * (1.0 + gate_proj * (1.0 - sigmoid_gate))).astype(
        narrow_number_type
    )
    d_up = (d_hidden * gate_proj * sigmoid_gate).astype(narrow_number_type)
    second_normalized_gradient = jnp.einsum(
        "bf,df->bd", d_gate, gate_w, preferred_element_type=wide_number_type
    ) + jnp.einsum("bf,df->bd", d_up, up_w, preferred_element_type=wide_number_type)
    gate_and_up = jnp.concatenate([d_gate, d_up], axis=1)
    both_sum = lax.psum_scatter(
        column_product(second_normalized, gate_and_up),
        ("dp", "ctx"),
        scatter_dimension=0,
        tiled=True,
    )
    gate_sum = both_sum[:, :FF]
    up_sum = both_sum[:, FF:]
    feedforward_gain_part = jnp.sum(second_normalized_gradient * second_standardized, axis=0)
    middle_gradient = d_out.astype(wide_number_type) + norm_backward(
        second_normalized_gradient,
        second_standardized,
        feedforward_gain.astype(wide_number_type),
        second_inverse_norm,
    )
    query_w, key_matrix, value_w, out_w, attention_gain = (
        lax.all_gather(w_query.astype(narrow_number_type), ("dp", "ctx"), axis=0, tiled=True),
        lax.all_gather(key_weight.astype(narrow_number_type), ("dp", "ctx"), axis=0, tiled=True),
        lax.all_gather(value_weight.astype(narrow_number_type), ("dp", "ctx"), axis=0, tiled=True),
        lax.all_gather(w_out.astype(narrow_number_type), ("dp", "ctx"), axis=0, tiled=True),
        lax.all_gather(
            attention_norm_gain.astype(narrow_number_type), ("dp", "ctx"), axis=0, tiled=True
        ),
    )
    d_branch = middle_gradient.astype(narrow_number_type)
    out_sum = lax.psum_scatter(
        column_product(attn_out, d_branch), ("dp", "ctx"), scatter_dimension=0, tiled=True
    )
    attention_gradient = jnp.einsum(
        "bd,hd->bh", d_branch, out_w, preferred_element_type=wide_number_type
    ).astype(narrow_number_type)
    attention_group_gradient = attention_gradient.reshape(
        token_rows, KEY_VALUE_HEADS, query_group_width, HEAD_SIZE
    )
    delta_rows = jnp.transpose(
        jnp.sum(attention_group_gradient.astype(wide_number_type) * attention_result, axis=-1),
        (1, 2, 0),
    )
    gathered_keys, gathered_values = (
        lax.all_gather(rotated_keys, "ctx", axis=0, tiled=True),
        lax.all_gather(value_rows, "ctx", axis=0, tiled=True),
    )
    count_of_blocks = gathered_keys.shape[0] // token_rows
    stacked_key_blocks = gathered_keys.reshape(
        count_of_blocks, token_rows, KEY_VALUE_HEADS * HEAD_SIZE
    )
    stacked_value_blocks = gathered_values.reshape(
        count_of_blocks, token_rows, KEY_VALUE_HEADS, HEAD_SIZE
    )

    def back_step(d_query_sum, block_item):
        current_key_block, value_block, block_index = block_item
        scores = masked_scores(current_key_block, block_index * token_rows)
        soft_part = jnp.exp(scores - log_total[..., None])
        d_value_block = jnp.einsum(
            "kgbj,bkgd->jkd",
            soft_part.astype(narrow_number_type),
            attention_group_gradient,
            preferred_element_type=wide_number_type,
        )
        d_probs = jnp.einsum(
            "bkgd,jkd->kgbj",
            attention_group_gradient,
            value_block,
            preferred_element_type=wide_number_type,
        )
        d_scores = (soft_part * (d_probs - delta_rows[..., None])).astype(narrow_number_type)
        key_tensor_triple = current_key_block.reshape(token_rows, KEY_VALUE_HEADS, HEAD_SIZE)
        d_query_sum = d_query_sum + jnp.einsum(
            "kgbj,jkd->bkgd", d_scores, key_tensor_triple, preferred_element_type=wide_number_type
        )
        d_key_block = jnp.einsum(
            "kgbj,bkgd->jkd", d_scores, grouped_queries, preferred_element_type=wide_number_type
        )
        return (d_query_sum, (d_key_block, d_value_block))

    d_query_sum, (key_gradients, value_gradients) = lax.scan(
        back_step,
        jnp.zeros((token_rows, KEY_VALUE_HEADS, query_group_width, HEAD_SIZE), wide_number_type),
        (stacked_key_blocks, stacked_value_blocks, jnp.arange(count_of_blocks, dtype=jnp.int32)),
    )
    key_gradients = (
        key_gradients.reshape(count_of_blocks * token_rows, KEY_VALUE_HEADS * HEAD_SIZE)
        * attention_score_scale
    )
    value_gradients = value_gradients.reshape(
        count_of_blocks * token_rows, KEY_VALUE_HEADS * HEAD_SIZE
    )
    local_keys, own_values = (
        lax.psum_scatter(
            key_gradients.astype(jnp.bfloat16), "ctx", scatter_dimension=0, tiled=True
        ).astype(jnp.float32),
        lax.psum_scatter(
            value_gradients.astype(jnp.bfloat16), "ctx", scatter_dimension=0, tiled=True
        ).astype(jnp.float32),
    )
    d_key = (
        reverse_rotary(
            local_keys.reshape(token_rows, KEY_VALUE_HEADS, HEAD_SIZE), cosine_table, sines_lookup
        )
        .reshape(token_rows, KEY_VALUE_HEADS * HEAD_SIZE)
        .astype(narrow_number_type)
    )
    d_value = own_values.astype(narrow_number_type)
    d_query = reverse_rotary(
        (d_query_sum * attention_score_scale).reshape(token_rows, QUERY_HEADS, HEAD_SIZE),
        cosine_table,
        sines_lookup,
    )
    d_query = d_query.reshape(token_rows, QUERY_HEADS * HEAD_SIZE).astype(narrow_number_type)
    d_projected = jnp.concatenate([d_query, d_key, d_value], axis=1)
    projection_total = lax.psum_scatter(
        column_product(first_normalized, d_projected),
        ("dp", "ctx"),
        scatter_dimension=0,
        tiled=True,
    )
    query_sum = projection_total[:, : QUERY_HEADS * HEAD_SIZE]
    key_gradient_sum = projection_total[
        :, QUERY_HEADS * HEAD_SIZE : QUERY_HEADS * HEAD_SIZE + KEY_VALUE_HEADS * HEAD_SIZE
    ]
    value_gradient_sum = projection_total[
        :, QUERY_HEADS * HEAD_SIZE + KEY_VALUE_HEADS * HEAD_SIZE :
    ]
    first_normalized_gradient = (
        jnp.einsum("bh,dh->bd", d_query, query_w, preferred_element_type=wide_number_type)
        + jnp.einsum("bh,dh->bd", d_key, key_matrix, preferred_element_type=wide_number_type)
        + jnp.einsum("bh,dh->bd", d_value, value_w, preferred_element_type=wide_number_type)
    )
    attention_gain_part = jnp.sum(first_normalized_gradient * first_standardized, axis=0)
    gradient_of_input = middle_gradient + norm_backward(
        first_normalized_gradient,
        first_standardized,
        attention_gain.astype(wide_number_type),
        first_inverse_norm,
    )
    attn_gain_sum, mlp_gain_sum = (
        lax.psum_scatter(attention_gain_part, ("dp", "ctx"), scatter_dimension=0, tiled=True),
        lax.psum_scatter(feedforward_gain_part, ("dp", "ctx"), scatter_dimension=0, tiled=True),
    )
    input_grad = gradient_of_input.astype(narrow_number_type)[None]
    return (
        output,
        input_grad,
        query_sum,
        key_gradient_sum,
        value_gradient_sum,
        out_sum,
        gate_sum,
        up_sum,
        down_sum,
        attn_gain_sum,
        mlp_gain_sum,
    )

N_Z = 4


def after(value, *others):
    return lax.optimization_barrier((value,) + others)[0]


def swap_cores(values):
    return lax.ppermute(values, "ctx", [(i, i ^ 1) for i in range(2 * N_Z)])


def gather_ctx(rows):
    return lax.all_gather(rows, "ctx", axis=0, tiled=True)


def scatter_ctx(partial):
    return lax.psum_scatter(partial, "ctx", scatter_dimension=0, tiled=True).astype(jnp.float32)


def hop(values, lowest, highest):
    moves = [(2 * z, 2 * z + 2) for z in range(lowest, highest + 1)]
    moves += [(2 * (N_Z - 1 - z) + 1, 2 * (N_Z - 1 - z) - 1) for z in range(lowest, highest + 1)]
    return lax.ppermute(values, "ctx", moves)


def pass_along(rows, *first):
    other = swap_cores(rows)
    even = is_even()
    pair = jnp.concatenate([jnp.where(even, rows, other), jnp.where(even, other, rows)], axis=0)
    held = [after(pair, *first)]
    for step in range(1, N_Z):
        held.append(hop(held[-1], step - 1, N_Z - 2))
    return held


def place_passed(held):
    z, even = lax.axis_index("ctx") // 2, is_even()
    size = held[0].shape[0]
    whole = jnp.zeros(((N_Z + 1) * size,) + held[0].shape[1:], held[0].dtype)
    whole = lax.dynamic_update_slice_in_dim(whole, held[0], z * size, 0)
    for step in range(1, N_Z):
        for block, up in ((held[step], even), (swap_cores(held[step]), ~even)):
            place = jnp.where(up, z - step, z + step)
            place = jnp.where((place >= 0) & (place < N_Z), place, N_Z)
            whole = lax.dynamic_update_slice_in_dim(whole, block, place * size, 0)
    return whole[: N_Z * size]


def send_dp(values, first, second):
    moves = [(d, c, d ^ (second if c % 2 else first)) for d in range(4) for c in range(2 * N_Z)]
    moves = [(d * 2 * N_Z + c, to * 2 * N_Z + c) for d, c, to in moves]
    return lax.ppermute(values, ("dp", "ctx"), moves)


def rotate_z(values, step):
    moves = [(2 * a + t, 2 * ((a + step) % N_Z) + t) for a in range(N_Z) for t in range(2)]
    return lax.ppermute(values, "ctx", moves)


def is_even():
    return lax.axis_index("ctx") % 2 == 0


def near_bit():
    return jnp.where(is_even(), 1, 2)


def place_dp(rows, first, second, third):
    d = lax.axis_index("dp")
    size = rows.shape[0]
    whole = jnp.zeros((4 * size,) + rows.shape[1:], rows.dtype)
    for block, place in (
        (rows, d),
        (first, d ^ near_bit()),
        (second, d ^ (3 - near_bit())),
        (third, d ^ 3),
    ):
        whole = lax.dynamic_update_slice_in_dim(whole, block, place * size, 0)
    return whole


def stack_dp(rows, first, second, third):
    one = jnp.where(is_even(), first, second)
    two = jnp.where(is_even(), second, first)
    return jnp.concatenate([rows, one, two, third], axis=0)


def pick(blocks, chip, core):
    start = (chip, core) + (0,) * (blocks.ndim - 2)
    return lax.dynamic_slice(blocks, start, (1, 1) + blocks.shape[2:])[0, 0]


def exchange_pairs(blocks):
    z, core = lax.axis_index("ctx") // 2, lax.axis_index("ctx") % 2
    give = jnp.stack([pick(blocks, (z + s) % N_Z, 1 - core) for s in range(N_Z)])
    got = swap_cores(give)
    pairs = []
    for s in range(N_Z):
        keep = pick(blocks, (z + s) % N_Z, core)
        pairs.append(
            jnp.concatenate(
                [jnp.where(is_even(), keep, got[s]), jnp.where(is_even(), got[s], keep)], axis=0
            )
        )
    return pairs


def place_z(pieces):
    z = lax.axis_index("ctx") // 2
    size = pieces[0].shape[0]
    whole = jnp.zeros((N_Z * size,) + pieces[0].shape[1:], pieces[0].dtype)
    for s, piece in enumerate(pieces):
        whole = lax.dynamic_update_slice_in_dim(whole, piece, (z - s) % N_Z * size, 0)
    return whole


def rotate_pieces(pairs):
    return [pairs[0]] + [rotate_z(pairs[s], s) for s in range(1, N_Z)]


def out_weight_moves():
    moves = []
    for block in range(8 * N_Z):
        head, part = divmod(block, N_Z)
        moves.append((block, part * 2 * N_Z + head))
    return moves


def head_local(
    layer_input,
    cotangent,
    prefix,
    w_query,
    key_weight,
    value_weight,
    w_out,
    w_gate,
    w_up,
    w_down,
    attention_norm_gain,
    feedforward_norm_gain,
):
    low = jnp.bfloat16
    wide = jnp.float32
    d = lax.axis_index("dp")
    even = is_even()
    rows = w_query.shape[0]
    seq_rows = layer_input.shape[1] * 2 * N_Z
    ff_part = w_down.shape[0]
    width = 4 * ff_part
    cols = 2 * HEAD_SIZE

    def dot(left, right):
        return jnp.dot(left, right, preferred_element_type=wide)

    def dot_t(left, right):
        return lax.dot_general(left, right, (((1,), (1,)), ((), ())), preferred_element_type=wide)

    def t_dot(left, right):
        return lax.dot_general(left, right, (((0,), (0,)), ((), ())), preferred_element_type=wide)

    def lowered(weight):
        return weight.astype(low).astype(wide)

    def turned(values):
        size = values.shape[1] // 4
        return jnp.concatenate(
            [lax.dynamic_slice_in_dim(values, (d ^ e) * size, size, 1) for e in range(4)], axis=1
        )

    def block_columns(values, e):
        size = values.shape[1] // 4
        return lax.dynamic_slice_in_dim(values, e * size, size, 1)

    x_rows = layer_input[0].astype(wide)
    d_out = cotangent[0]
    gain_a = lowered(attention_norm_gain)[:, None]
    gain_m = lowered(feedforward_norm_gain)[:, None]
    low_q, low_k, low_v = lowered(w_query), lowered(key_weight), lowered(value_weight)
    low_g, low_u = lowered(w_gate), lowered(w_up)

    moves = out_weight_moves()
    out_own = lax.ppermute(w_out.astype(low), ("dp", "ctx"), moves)

    inverse1 = lax.rsqrt(jnp.mean(x_rows * x_rows, axis=-1, keepdims=True) + NORM_EPSILON)
    hat1 = x_rows * inverse1
    sent1 = turned(hat1).astype(low)

    q_cols = (low_q * gain_a).astype(low).reshape(rows, N_Z, 2, HEAD_SIZE).transpose(1, 2, 0, 3)
    k_cols = (low_k * gain_a).astype(low).reshape(rows, N_Z, 1, HEAD_SIZE).transpose(1, 2, 0, 3)
    v_cols = (low_v * gain_a).astype(low).reshape(rows, N_Z, 1, HEAD_SIZE).transpose(1, 2, 0, 3)
    proj_blocks = jnp.concatenate([q_cols, jnp.concatenate([k_cols, v_cols], axis=1)], axis=3)
    proj_pairs = exchange_pairs(proj_blocks)
    proj_moved = rotate_pieces(proj_pairs)
    all_hat1 = gather_ctx(sent1)
    proj_own = place_z(proj_moved)
    proj_first, proj_second = send_dp(proj_own, 1, 2), send_dp(proj_own, 2, 1)
    proj_third = send_dp(proj_first, 2, 1)
    gain_late = after(gain_m, *proj_pairs)

    def ff_columns(weight):
        blocks = (weight * gain_late).astype(low).reshape(rows, 4, N_Z, 2, ff_part)
        return blocks.transpose(2, 3, 0, 1, 4).reshape(N_Z, 2, rows, width)

    gate_up_pairs = exchange_pairs(jnp.concatenate([ff_columns(low_g), ff_columns(low_u)], axis=3))
    down_own = w_down.astype(low)
    all_hat1, proj_third, out_own, down_own, *gate_up_pairs = lax.optimization_barrier(
        (all_hat1, proj_third, out_own, down_own, *gate_up_pairs)
    )
    out_first, out_second = send_dp(out_own, 1, 2), send_dp(out_own, 2, 1)
    out_w = place_dp(out_own, out_first, out_second, send_dp(out_first, 2, 1))
    down_first, down_second = send_dp(down_own, 1, 2), send_dp(down_own, 2, 1)
    all_cot = gather_ctx(after(d_out, all_hat1))
    proj = stack_dp(proj_own, proj_first, proj_second, proj_third)
    gate_up_moved = rotate_pieces(gate_up_pairs)
    positions = jnp.arange(seq_rows, dtype=jnp.int32)
    cosine, sine = rope_angles(positions, HEAD_SIZE)
    cosine, sine = cosine[:, 0], sine[:, 0]
    half = HEAD_SIZE // 2

    def rotate(v, turn):
        a, b = v[:, :half], v[:, half:]
        return jnp.concatenate([a * cosine - turn * b * sine, b * cosine + turn * a * sine], axis=1)

    qkv = dot(all_hat1, proj)
    scale = HEAD_SIZE ** (-0.5)
    q_rot = (rotate(qkv[:, :HEAD_SIZE], 1.0) * scale).astype(low)
    own = qkv[:, HEAD_SIZE:]
    own = jnp.where(even, rotate(own, 1.0), own).astype(low)
    other = swap_cores(own)
    keys = jnp.where(even, own, other)
    values = jnp.where(even, other, own)
    allowed = (positions[None, :] <= positions[:, None]) | (positions[None, :] < prefix[0])
    scores = jnp.where(allowed, dot_t(q_rot, keys), -1e30)
    peak = jnp.max(scores, axis=-1, keepdims=True)
    weights = jnp.exp(scores - peak)
    total = jnp.sum(weights, axis=-1, keepdims=True)
    attended = dot(weights.astype(low), values) / total
    attn = attended.astype(low)
    branch_part = dot(attn, out_w).astype(low)
    branch_part, down_first, down_second, all_cot, *gate_up_moved = lax.optimization_barrier(
        (branch_part, down_first, down_second, all_cot, *gate_up_moved)
    )
    gate_up_own = place_z(gate_up_moved)
    branch = scatter_ctx(branch_part)
    gu_first, gu_second = send_dp(gate_up_own, 1, 2), send_dp(gate_up_own, 2, 1)
    middle = x_rows + branch

    inverse2 = lax.rsqrt(jnp.mean(middle * middle, axis=-1, keepdims=True) + NORM_EPSILON)
    hat2 = middle * inverse2
    sent2, gu_first, gu_second = lax.optimization_barrier(
        (turned(hat2).astype(low), gu_first, gu_second)
    )
    all_hat2 = gather_ctx(sent2)
    gu_third = send_dp(gu_first, 2, 1)
    down_third = send_dp(after(down_first, gu_first), 2, 1)
    gate_up_w = stack_dp(gate_up_own, gu_first, gu_second, gu_third)
    down_w = place_dp(down_own, down_first, down_second, down_third)
    d_hidden = dot_t(all_cot, down_w)
    all_hat2, gate_up_w, down_w, all_cot, d_hidden = lax.optimization_barrier(
        (all_hat2, gate_up_w, down_w, all_cot, d_hidden)
    )
    gate = dot(all_hat2, gate_up_w[:, :width])
    up = dot(all_hat2, gate_up_w[:, width:])
    sig = jax.nn.sigmoid(gate)
    silu = gate * sig
    hidden = (silu * up).astype(low)

    d_gate = (d_hidden * up * sig * (1.0 + gate * (1.0 - sig))).astype(low)
    d_up = (d_hidden * silu).astype(low)
    d_gate_up = jnp.concatenate([d_gate, d_up], axis=1)
    e2_part = dot_t(d_gate_up, gate_up_w).astype(low)
    e2 = scatter_ctx(e2_part)
    d_gate_up, hidden = lax.optimization_barrier((d_gate_up, hidden, e2_part))[:2]

    def gu_block(j):
        return t_dot(block_columns(all_hat2, j), d_gate_up)

    def down_block(j):
        return t_dot(block_columns(hidden, d ^ j), all_cot)

    gu_across = send_dp(gu_block(3).astype(low), 2, 1)
    gu_far = send_dp(gu_block(3 - near_bit()).astype(low), 2, 1)
    gu_near_term, gu_own_term = gu_block(near_bit()), gu_block(0)
    out_part = dot(hidden, down_w).astype(low)
    down_sent3 = down_block(3).astype(low)
    down_sent_far = down_block(3 - near_bit()).astype(low)
    e2, gu_across, gu_far, down_sent3, down_sent_far, out_part = lax.optimization_barrier(
        (e2, gu_across, gu_far, down_sent3, down_sent_far, out_part)
    )
    gu_near = send_dp((gu_near_term + gu_across.astype(wide)).astype(low), 1, 2)
    down_across, down_far = send_dp(down_sent3, 2, 1), send_dp(down_sent_far, 2, 1)
    e2 = turned(e2)
    d_middle = d_out.astype(wide) + inverse2 * (
        e2 - hat2 * jnp.mean(e2 * hat2, axis=-1, keepdims=True)
    )
    branch_low = d_middle.astype(low)
    out_branch = scatter_ctx(after(out_part, branch_low))
    all_branch = place_passed(pass_along(branch_low))
    gate_up_sum = (gu_own_term + gu_far.astype(wide) + gu_near.astype(wide)).astype(low)
    sum_pairs = exchange_pairs(gate_up_sum.reshape(N_Z, 2, rows, 2 * width))

    all_branch, down_across, down_far, out_branch, *sum_pairs = lax.optimization_barrier(
        (all_branch, down_across, down_far, out_branch, *sum_pairs)
    )
    head_part = t_dot(attn, all_branch)

    def out_block(j):
        return lax.dynamic_slice_in_dim(head_part, (d ^ j) * rows, rows, 0)

    out_across = send_dp(out_block(3).astype(low), 2, 1)
    out_far = send_dp(out_block(3 - near_bit()).astype(low), 2, 1)
    out_near = send_dp((out_block(near_bit()) + out_across.astype(wide)).astype(low), 1, 2)
    down_near = send_dp((down_block(near_bit()) + down_across.astype(wide)).astype(low), 1, 2)
    down_sum = down_block(0) + down_far.astype(wide) + down_near.astype(wide)
    gate_up_sum = place_z(rotate_pieces(sum_pairs))
    d_attn = dot_t(all_branch, out_w).astype(low)
    delta = jnp.sum(d_attn.astype(wide) * attended, axis=-1, keepdims=True)
    probs = weights / total
    d_scores = (probs * (dot_t(d_attn, values) - delta)).astype(low)
    d_query = rotate(dot(d_scores, keys) * scale, -1.0)
    dk_part = t_dot(d_scores, q_rot)
    dv_part = t_dot(probs.astype(low), d_attn)
    mine = jnp.where(even, dk_part, dv_part)
    mine = mine + swap_cores(jnp.where(even, dv_part, dk_part).astype(low)).astype(wide)
    mine = jnp.where(even, rotate(mine, -1.0), mine)
    d_proj = jnp.concatenate([d_query, mine], axis=1).astype(low)
    e1_part = dot_t(d_proj, proj).astype(low)
    e1 = turned(scatter_ctx(e1_part))
    d_proj, out_near = lax.optimization_barrier((d_proj, out_near, e1_part))[:2]
    output = (middle + out_branch).astype(low)[None]

    def proj_block(j):
        return t_dot(block_columns(all_hat1, j), d_proj)

    proj_across = send_dp(proj_block(3).astype(low), 2, 1)
    proj_far = send_dp(proj_block(3 - near_bit()).astype(low), 2, 1)
    proj_near = send_dp((proj_block(near_bit()) + proj_across.astype(wide)).astype(low), 1, 2)
    proj_sum = proj_block(0) + proj_far.astype(wide) + proj_near.astype(wide)
    proj_sum = place_z(
        rotate_pieces(exchange_pairs(proj_sum.astype(low).reshape(N_Z, 2, rows, cols)))
    )
    out_sum = out_block(0) + out_far.astype(wide) + out_near.astype(wide)
    out_sum = lax.ppermute(
        out_sum.astype(low), ("dp", "ctx"), [(to, start) for start, to in moves]
    ).astype(wide)

    def ff_rows(part):
        blocks = part.astype(wide).reshape(2 * N_Z, rows, 4, ff_part).transpose(1, 2, 0, 3)
        return blocks.reshape(rows, 8 * N_Z * ff_part)

    raw_gate = ff_rows(gate_up_sum[:, :width])
    raw_up = ff_rows(gate_up_sum[:, width:])
    gain_mlp = jnp.sum(raw_gate * low_g, axis=1) + jnp.sum(raw_up * low_u, axis=1)
    gate_sum, up_sum = raw_gate * gain_m, raw_up * gain_m
    proj_sum = proj_sum.astype(wide).reshape(2 * N_Z, rows, cols).transpose(1, 0, 2)
    raw_q = proj_sum[:, :, :HEAD_SIZE].reshape(rows, QUERY_HEADS * HEAD_SIZE)
    kv_sum = proj_sum[:, :, HEAD_SIZE:].reshape(rows, KEY_VALUE_HEADS, 2, HEAD_SIZE)
    raw_k = kv_sum[:, :, 0].reshape(rows, KEY_VALUE_HEADS * HEAD_SIZE)
    raw_v = kv_sum[:, :, 1].reshape(rows, KEY_VALUE_HEADS * HEAD_SIZE)
    gain_attn = (
        jnp.sum(raw_q * low_q, axis=1)
        + jnp.sum(raw_k * low_k, axis=1)
        + jnp.sum(raw_v * low_v, axis=1)
    )
    d_input = d_middle + inverse1 * (e1 - hat1 * jnp.mean(e1 * hat1, axis=-1, keepdims=True))
    return (
        output,
        d_input.astype(low)[None],
        raw_q * gain_a,
        raw_k * gain_a,
        raw_v * gain_a,
        out_sum,
        gate_sum,
        up_sum,
        down_sum,
        gain_attn,
        gain_mlp,
    )


def solution(mesh):
    local = head_local if (mesh.shape["dp"], mesh.shape["ctx"]) == (4, 2 * N_Z) else gathered_local
    in_specs = (
        P("dp", "ctx", None),
        P("dp", "ctx", None),
        P("dp"),
        P(("dp", "ctx"), None),
        P(("dp", "ctx"), None),
        P(("dp", "ctx"), None),
        P(("dp", "ctx"), None),
        P(("dp", "ctx"), None),
        P(("dp", "ctx"), None),
        P(("dp", "ctx"), None),
        P(("dp", "ctx")),
        P(("dp", "ctx")),
    )
    out_specs = (
        P("dp", "ctx", None),
        P("dp", "ctx", None),
        P(("dp", "ctx"), None),
        P(("dp", "ctx"), None),
        P(("dp", "ctx"), None),
        P(("dp", "ctx"), None),
        P(("dp", "ctx"), None),
        P(("dp", "ctx"), None),
        P(("dp", "ctx"), None),
        P(("dp", "ctx")),
        P(("dp", "ctx")),
    )
    return jax.shard_map(local, mesh=mesh, in_specs=in_specs, out_specs=out_specs, check_vma=False)
```

```python
import jax
import jax.numpy as jnp
from jax import lax
from jax.experimental import pallas as pl
from jax.experimental.pallas import tpu as pltpu
from jax.sharding import PartitionSpec as P

FF = 8192
QUERY_HEADS = 8
KEY_VALUE_HEADS = 4
HEAD_SIZE = 256


NORM_EPSILON = 1e-06
THETA = 1000042.0


def rope_angles(token_positions, width):
    half_width = width // 2
    frequency = jnp.power(THETA, -(2.0 * jnp.arange(half_width, dtype=jnp.float32) / width))
    angles = token_positions.astype(jnp.float32)[:, None] * frequency[None, :]
    return (jnp.cos(angles)[:, None, :], jnp.sin(angles)[:, None, :])


def apply_rotary(vector, cosine_table, sines_lookup):
    half_width = vector.shape[-1] // 2
    first_half = vector[..., :half_width]
    second_half = vector[..., half_width:]
    return jnp.concatenate(
        [
            first_half * cosine_table - second_half * sines_lookup,
            second_half * cosine_table + first_half * sines_lookup,
        ],
        axis=-1,
    )


def reverse_rotary(vector, cosine_table, sines_lookup):
    half_width = vector.shape[-1] // 2
    first_half = vector[..., :half_width]
    second_half = vector[..., half_width:]
    return jnp.concatenate(
        [
            first_half * cosine_table + second_half * sines_lookup,
            second_half * cosine_table - first_half * sines_lookup,
        ],
        axis=-1,
    )


def norm_backward(d_normed, hat_values, gain_row, inverse):
    scaled = d_normed * gain_row
    return inverse * (scaled - hat_values * jnp.mean(scaled * hat_values, axis=-1, keepdims=True))


def column_product(left, right):
    return jnp.einsum("bd,bf->df", left, right, preferred_element_type=jnp.float32)


def gathered_local(
    layer_input,
    cotangent,
    prefix,
    w_query,
    key_weight,
    value_weight,
    w_out,
    w_gate,
    w_up,
    w_down,
    attention_norm_gain,
    feedforward_norm_gain,
):
    narrow_number_type = jnp.bfloat16
    wide_number_type = jnp.float32
    token_rows = layer_input.shape[1]
    query_group_width = QUERY_HEADS // KEY_VALUE_HEADS
    attention_score_scale = HEAD_SIZE ** (-0.5)
    input_rows_all = layer_input[0].astype(wide_number_type)
    first_row = lax.axis_index("ctx") * token_rows
    token_positions = first_row + jnp.arange(token_rows, dtype=jnp.int32)
    prefix_len = prefix[0]
    cosine_table, sines_lookup = rope_angles(token_positions, HEAD_SIZE)
    attn_kept = (
        lax.all_gather(w_query.astype(narrow_number_type), ("dp", "ctx"), axis=0, tiled=True),
        lax.all_gather(key_weight.astype(narrow_number_type), ("dp", "ctx"), axis=0, tiled=True),
        lax.all_gather(value_weight.astype(narrow_number_type), ("dp", "ctx"), axis=0, tiled=True),
        lax.all_gather(w_out.astype(narrow_number_type), ("dp", "ctx"), axis=0, tiled=True),
        lax.all_gather(
            attention_norm_gain.astype(narrow_number_type), ("dp", "ctx"), axis=0, tiled=True
        ),
    )
    query_w, key_matrix, value_w, out_w, attention_gain = attn_kept
    first_inverse_norm = lax.rsqrt(
        jnp.mean(input_rows_all * input_rows_all, axis=-1, keepdims=True) + NORM_EPSILON
    )
    first_standardized = input_rows_all * first_inverse_norm
    first_normalized = (first_standardized * attention_gain.astype(wide_number_type)).astype(
        narrow_number_type
    )
    query_rows = jnp.dot(
        first_normalized, query_w, preferred_element_type=wide_number_type
    ).reshape(token_rows, QUERY_HEADS, HEAD_SIZE)
    projected_keys = jnp.dot(
        first_normalized, key_matrix, preferred_element_type=wide_number_type
    ).reshape(token_rows, KEY_VALUE_HEADS, HEAD_SIZE)
    value_rows = jnp.dot(first_normalized, value_w, preferred_element_type=wide_number_type).astype(
        narrow_number_type
    )
    rotated_queries = apply_rotary(query_rows, cosine_table, sines_lookup).astype(
        narrow_number_type
    )
    rotated_keys = (
        apply_rotary(projected_keys, cosine_table, sines_lookup)
        .astype(narrow_number_type)
        .reshape(token_rows, KEY_VALUE_HEADS * HEAD_SIZE)
    )
    grouped_queries = rotated_queries.reshape(
        token_rows, KEY_VALUE_HEADS, query_group_width, HEAD_SIZE
    )

    def masked_scores(key_segment, start_row):
        segment_rows = key_segment.shape[0]
        columns = start_row + jnp.arange(segment_rows, dtype=jnp.int32)
        allowed = (columns[None, :] <= token_positions[:, None]) | (columns[None, :] < prefix_len)
        scores = (
            jnp.einsum(
                "bkgd,jkd->kgbj",
                grouped_queries,
                key_segment.reshape(segment_rows, KEY_VALUE_HEADS, HEAD_SIZE),
                preferred_element_type=wide_number_type,
            )
            * attention_score_scale
        )
        return jnp.where(allowed[None, None], scores, -jnp.inf)

    row_maximum = jnp.full(
        (KEY_VALUE_HEADS, query_group_width, token_rows), -1e30, wide_number_type
    )
    key_segment = lax.all_gather(rotated_keys, "ctx", axis=0, tiled=True)
    value_segment = lax.all_gather(value_rows, "ctx", axis=0, tiled=True)
    segment_rows = value_segment.shape[0]
    scores = masked_scores(key_segment, jnp.int32(0))
    new_peak = jnp.maximum(row_maximum, jnp.max(scores, axis=-1))
    soft_part = jnp.exp(scores - new_peak[..., None])
    row_denominator = jnp.sum(soft_part, axis=-1)
    weighted_values = jnp.einsum(
        "kgbj,jkd->bkgd",
        soft_part.astype(narrow_number_type),
        value_segment.reshape(segment_rows, KEY_VALUE_HEADS, HEAD_SIZE),
        preferred_element_type=wide_number_type,
    )
    row_maximum, row_denominator, weighted_values = (new_peak, row_denominator, weighted_values)
    log_total = row_maximum + jnp.log(row_denominator)
    attention_result = weighted_values / jnp.transpose(row_denominator, (2, 0, 1))[..., None]
    attn_out = attention_result.reshape(token_rows, QUERY_HEADS * HEAD_SIZE).astype(
        narrow_number_type
    )
    hidden_middle = input_rows_all + jnp.dot(
        attn_out, out_w, preferred_element_type=wide_number_type
    )
    mlp_kept = (
        lax.all_gather(w_gate.astype(narrow_number_type), ("dp", "ctx"), axis=0, tiled=True),
        lax.all_gather(w_up.astype(narrow_number_type), ("dp", "ctx"), axis=0, tiled=True),
        lax.all_gather(w_down.astype(narrow_number_type), ("dp", "ctx"), axis=0, tiled=True),
        lax.all_gather(
            feedforward_norm_gain.astype(narrow_number_type), ("dp", "ctx"), axis=0, tiled=True
        ),
    )
    gate_w, up_w, down_w, feedforward_gain = mlp_kept
    second_inverse_norm = lax.rsqrt(
        jnp.mean(hidden_middle * hidden_middle, axis=-1, keepdims=True) + NORM_EPSILON
    )
    second_standardized = hidden_middle * second_inverse_norm
    second_normalized = (second_standardized * feedforward_gain.astype(wide_number_type)).astype(
        narrow_number_type
    )
    gate_proj = jnp.dot(second_normalized, gate_w, preferred_element_type=wide_number_type)
    up_proj = jnp.dot(second_normalized, up_w, preferred_element_type=wide_number_type)
    hidden = (jax.nn.silu(gate_proj) * up_proj).astype(narrow_number_type)
    result = hidden_middle + jnp.dot(hidden, down_w, preferred_element_type=wide_number_type)
    output = result.astype(narrow_number_type)[None]
    gate_w, up_w, down_w, feedforward_gain = (
        lax.all_gather(w_gate.astype(narrow_number_type), ("dp", "ctx"), axis=0, tiled=True),
        lax.all_gather(w_up.astype(narrow_number_type), ("dp", "ctx"), axis=0, tiled=True),
        lax.all_gather(w_down.astype(narrow_number_type), ("dp", "ctx"), axis=0, tiled=True),
        lax.all_gather(
            feedforward_norm_gain.astype(narrow_number_type), ("dp", "ctx"), axis=0, tiled=True
        ),
    )
    d_out = cotangent[0]
    down_sum = lax.psum_scatter(
        column_product(hidden, d_out), ("dp", "ctx"), scatter_dimension=0, tiled=True
    )
    d_hidden = jnp.einsum("bd,fd->bf", d_out, down_w, preferred_element_type=wide_number_type)
    sigmoid_gate = jax.nn.sigmoid(gate_proj)
    d_gate = (d_hidden * up_proj * sigmoid_gate * (1.0 + gate_proj * (1.0 - sigmoid_gate))).astype(
        narrow_number_type
    )
    d_up = (d_hidden * gate_proj * sigmoid_gate).astype(narrow_number_type)
    second_normalized_gradient = jnp.einsum(
        "bf,df->bd", d_gate, gate_w, preferred_element_type=wide_number_type
    ) + jnp.einsum("bf,df->bd", d_up, up_w, preferred_element_type=wide_number_type)
    gate_and_up = jnp.concatenate([d_gate, d_up], axis=1)
    both_sum = lax.psum_scatter(
        column_product(second_normalized, gate_and_up),
        ("dp", "ctx"),
        scatter_dimension=0,
        tiled=True,
    )
    gate_sum = both_sum[:, :FF]
    up_sum = both_sum[:, FF:]
    feedforward_gain_part = jnp.sum(second_normalized_gradient * second_standardized, axis=0)
    middle_gradient = d_out.astype(wide_number_type) + norm_backward(
        second_normalized_gradient,
        second_standardized,
        feedforward_gain.astype(wide_number_type),
        second_inverse_norm,
    )
    query_w, key_matrix, value_w, out_w, attention_gain = (
        lax.all_gather(w_query.astype(narrow_number_type), ("dp", "ctx"), axis=0, tiled=True),
        lax.all_gather(key_weight.astype(narrow_number_type), ("dp", "ctx"), axis=0, tiled=True),
        lax.all_gather(value_weight.astype(narrow_number_type), ("dp", "ctx"), axis=0, tiled=True),
        lax.all_gather(w_out.astype(narrow_number_type), ("dp", "ctx"), axis=0, tiled=True),
        lax.all_gather(
            attention_norm_gain.astype(narrow_number_type), ("dp", "ctx"), axis=0, tiled=True
        ),
    )
    d_branch = middle_gradient.astype(narrow_number_type)
    out_sum = lax.psum_scatter(
        column_product(attn_out, d_branch), ("dp", "ctx"), scatter_dimension=0, tiled=True
    )
    attention_gradient = jnp.einsum(
        "bd,hd->bh", d_branch, out_w, preferred_element_type=wide_number_type
    ).astype(narrow_number_type)
    attention_group_gradient = attention_gradient.reshape(
        token_rows, KEY_VALUE_HEADS, query_group_width, HEAD_SIZE
    )
    delta_rows = jnp.transpose(
        jnp.sum(attention_group_gradient.astype(wide_number_type) * attention_result, axis=-1),
        (1, 2, 0),
    )
    gathered_keys, gathered_values = (
        lax.all_gather(rotated_keys, "ctx", axis=0, tiled=True),
        lax.all_gather(value_rows, "ctx", axis=0, tiled=True),
    )
    count_of_blocks = gathered_keys.shape[0] // token_rows
    stacked_key_blocks = gathered_keys.reshape(
        count_of_blocks, token_rows, KEY_VALUE_HEADS * HEAD_SIZE
    )
    stacked_value_blocks = gathered_values.reshape(
        count_of_blocks, token_rows, KEY_VALUE_HEADS, HEAD_SIZE
    )

    def back_step(d_query_sum, block_item):
        current_key_block, value_block, block_index = block_item
        scores = masked_scores(current_key_block, block_index * token_rows)
        soft_part = jnp.exp(scores - log_total[..., None])
        d_value_block = jnp.einsum(
            "kgbj,bkgd->jkd",
            soft_part.astype(narrow_number_type),
            attention_group_gradient,
            preferred_element_type=wide_number_type,
        )
        d_probs = jnp.einsum(
            "bkgd,jkd->kgbj",
            attention_group_gradient,
            value_block,
            preferred_element_type=wide_number_type,
        )
        d_scores = (soft_part * (d_probs - delta_rows[..., None])).astype(narrow_number_type)
        key_tensor_triple = current_key_block.reshape(token_rows, KEY_VALUE_HEADS, HEAD_SIZE)
        d_query_sum = d_query_sum + jnp.einsum(
            "kgbj,jkd->bkgd", d_scores, key_tensor_triple, preferred_element_type=wide_number_type
        )
        d_key_block = jnp.einsum(
            "kgbj,bkgd->jkd", d_scores, grouped_queries, preferred_element_type=wide_number_type
        )
        return (d_query_sum, (d_key_block, d_value_block))

    d_query_sum, (key_gradients, value_gradients) = lax.scan(
        back_step,
        jnp.zeros((token_rows, KEY_VALUE_HEADS, query_group_width, HEAD_SIZE), wide_number_type),
        (stacked_key_blocks, stacked_value_blocks, jnp.arange(count_of_blocks, dtype=jnp.int32)),
    )
    key_gradients = (
        key_gradients.reshape(count_of_blocks * token_rows, KEY_VALUE_HEADS * HEAD_SIZE)
        * attention_score_scale
    )
    value_gradients = value_gradients.reshape(
        count_of_blocks * token_rows, KEY_VALUE_HEADS * HEAD_SIZE
    )
    local_keys, own_values = (
        lax.psum_scatter(
            key_gradients.astype(jnp.bfloat16), "ctx", scatter_dimension=0, tiled=True
        ).astype(jnp.float32),
        lax.psum_scatter(
            value_gradients.astype(jnp.bfloat16), "ctx", scatter_dimension=0, tiled=True
        ).astype(jnp.float32),
    )
    d_key = (
        reverse_rotary(
            local_keys.reshape(token_rows, KEY_VALUE_HEADS, HEAD_SIZE), cosine_table, sines_lookup
        )
        .reshape(token_rows, KEY_VALUE_HEADS * HEAD_SIZE)
        .astype(narrow_number_type)
    )
    d_value = own_values.astype(narrow_number_type)
    d_query = reverse_rotary(
        (d_query_sum * attention_score_scale).reshape(token_rows, QUERY_HEADS, HEAD_SIZE),
        cosine_table,
        sines_lookup,
    )
    d_query = d_query.reshape(token_rows, QUERY_HEADS * HEAD_SIZE).astype(narrow_number_type)
    d_projected = jnp.concatenate([d_query, d_key, d_value], axis=1)
    projection_total = lax.psum_scatter(
        column_product(first_normalized, d_projected),
        ("dp", "ctx"),
        scatter_dimension=0,
        tiled=True,
    )
    query_sum = projection_total[:, : QUERY_HEADS * HEAD_SIZE]
    key_gradient_sum = projection_total[
        :, QUERY_HEADS * HEAD_SIZE : QUERY_HEADS * HEAD_SIZE + KEY_VALUE_HEADS * HEAD_SIZE
    ]
    value_gradient_sum = projection_total[
        :, QUERY_HEADS * HEAD_SIZE + KEY_VALUE_HEADS * HEAD_SIZE :
    ]
    first_normalized_gradient = (
        jnp.einsum("bh,dh->bd", d_query, query_w, preferred_element_type=wide_number_type)
        + jnp.einsum("bh,dh->bd", d_key, key_matrix, preferred_element_type=wide_number_type)
        + jnp.einsum("bh,dh->bd", d_value, value_w, preferred_element_type=wide_number_type)
    )
    attention_gain_part = jnp.sum(first_normalized_gradient * first_standardized, axis=0)
    gradient_of_input = middle_gradient + norm_backward(
        first_normalized_gradient,
        first_standardized,
        attention_gain.astype(wide_number_type),
        first_inverse_norm,
    )
    attn_gain_sum, mlp_gain_sum = (
        lax.psum_scatter(attention_gain_part, ("dp", "ctx"), scatter_dimension=0, tiled=True),
        lax.psum_scatter(feedforward_gain_part, ("dp", "ctx"), scatter_dimension=0, tiled=True),
    )
    input_grad = gradient_of_input.astype(narrow_number_type)[None]
    return (
        output,
        input_grad,
        query_sum,
        key_gradient_sum,
        value_gradient_sum,
        out_sum,
        gate_sum,
        up_sum,
        down_sum,
        attn_gain_sum,
        mlp_gain_sum,
    )

N_Z = 4


def after(value, *others):
    return lax.optimization_barrier((value,) + others)[0]


def swap_cores(values):
    return lax.ppermute(values, "ctx", [(i, i ^ 1) for i in range(2 * N_Z)])


def gather_ctx(rows):
    return lax.all_gather(rows, "ctx", axis=0, tiled=True)


def scatter_ctx(partial):
    return lax.psum_scatter(partial, "ctx", scatter_dimension=0, tiled=True).astype(jnp.float32)


def hop(values, lowest, highest):
    moves = [(2 * z, 2 * z + 2) for z in range(lowest, highest + 1)]
    moves += [(2 * (N_Z - 1 - z) + 1, 2 * (N_Z - 1 - z) - 1) for z in range(lowest, highest + 1)]
    return lax.ppermute(values, "ctx", moves)


def sum_step(slots, carried, step):
    low, wide = jnp.bfloat16, jnp.float32
    keep = jnp.where(is_even(), slots[step], slots[N_Z - step])
    give = jnp.where(is_even(), slots[N_Z - step], slots[step])
    total = keep.astype(wide) + swap_cores(give).astype(wide)
    if carried is not None:
        total = total + carried.astype(wide)
    return hop(total.astype(low), 0, N_Z - 1 - step)


def sum_end(slots, carried):
    low, wide = jnp.bfloat16, jnp.float32
    total = slots[0].astype(wide) + carried.astype(wide)
    half = total.shape[0] // 2
    give = jnp.where(is_even(), total[half:], total[:half]).astype(low)
    return jnp.where(is_even(), total[:half], total[half:]) + swap_cores(give).astype(wide)


def send_dp(values, first, second):
    moves = [(d, c, d ^ (second if c % 2 else first)) for d in range(4) for c in range(2 * N_Z)]
    moves = [(d * 2 * N_Z + c, to * 2 * N_Z + c) for d, c, to in moves]
    return lax.ppermute(values, ("dp", "ctx"), moves)


def is_even():
    return lax.axis_index("ctx") % 2 == 0


def near_bit():
    return jnp.where(is_even(), 1, 2)


def place_dp(rows, first, second, third):
    d = lax.axis_index("dp")
    size = rows.shape[0]
    whole = jnp.zeros((4 * size,) + rows.shape[1:], rows.dtype)
    for block, place in (
        (rows, d),
        (first, d ^ near_bit()),
        (second, d ^ (3 - near_bit())),
        (third, d ^ 3),
    ):
        whole = lax.dynamic_update_slice_in_dim(whole, block, place * size, 0)
    return whole


def stack_dp(rows, first, second, third):
    one = jnp.where(is_even(), first, second)
    two = jnp.where(is_even(), second, first)
    return jnp.concatenate([rows, one, two, third], axis=0)


def exchange_ctx(blocks):
    return lax.all_to_all(blocks, "ctx", 0, 0, tiled=True)


def finish_feedforward(sums, w_gate, w_up, gain):
    n_ctx, rows, both = sums.shape
    part = both // 8

    def kernel(sums_ref, gate_ref, up_ref, gain_ref, gate_out, up_out, gain_out):
        scale = gain_ref[...]
        total = jnp.zeros((rows, part), jnp.float32)
        for d in range(4):
            for c in range(n_ctx):
                place = pl.ds((d * n_ctx + c) * part, part)
                for half, weight_ref, out_ref in ((0, gate_ref, gate_out), (1, up_ref, up_out)):
                    raw = sums_ref[c, :, pl.ds((half * 4 + d) * part, part)].astype(jnp.float32)
                    weight = weight_ref[:, place].astype(jnp.bfloat16).astype(jnp.float32)
                    total = total + raw * weight
                    out_ref[:, place] = raw * scale
        gain_out[...] = jnp.sum(total, axis=1, keepdims=True)

    return pl.pallas_call(
        kernel,
        out_shape=(
            jax.ShapeDtypeStruct(w_gate.shape, jnp.float32),
            jax.ShapeDtypeStruct(w_up.shape, jnp.float32),
            jax.ShapeDtypeStruct((rows, 1), jnp.float32),
        ),
        compiler_params=pltpu.CompilerParams(vmem_limit_bytes=32 * 1024 * 1024),
        cost_estimate=pl.CostEstimate(
            flops=4 * w_gate.size, bytes_accessed=20 * w_gate.size, transcendentals=0
        ),
    )(sums, w_gate, w_up, gain)


def feedforward(hat, weight, d_hidden):
    rows, depth = hat.shape
    width = weight.shape[1] // 2
    tile, chunk = 256, 256
    tiles = width // tile

    def kernel(hat_ref, gate_ref, up_ref, grad_ref, hidden_ref, out_ref):
        place = pl.multiple_of(pl.program_id(0) * tile, tile)
        for start in range(0, rows, chunk):
            part = pl.ds(start, chunk)
            left = hat_ref[part, :]
            gate = jnp.dot(left, gate_ref[...], preferred_element_type=jnp.float32)
            up = jnp.dot(left, up_ref[...], preferred_element_type=jnp.float32)
            sig = jax.nn.sigmoid(gate)
            silu = gate * sig
            grad = grad_ref[part, :]
            hidden_ref[part, :] = (silu * up).astype(jnp.bfloat16)
            d_gate = grad * up * sig * (1.0 + gate * (1.0 - sig))
            out_ref[part, pl.ds(place, tile)] = d_gate.astype(jnp.bfloat16)
            out_ref[part, pl.ds(width + place, tile)] = (grad * silu).astype(jnp.bfloat16)

    return pl.pallas_call(
        kernel,
        grid=(tiles,),
        in_specs=[
            pl.BlockSpec((rows, depth), lambda j: (0, 0)),
            pl.BlockSpec((depth, tile), lambda j: (0, j)),
            pl.BlockSpec((depth, tile), lambda j: (0, tiles + j)),
            pl.BlockSpec((rows, tile), lambda j: (0, j)),
        ],
        out_specs=(
            pl.BlockSpec((rows, tile), lambda j: (0, j)),
            pl.BlockSpec((rows, 2 * width), lambda j: (0, 0)),
        ),
        out_shape=(
            jax.ShapeDtypeStruct((rows, width), jnp.bfloat16),
            jax.ShapeDtypeStruct((rows, 2 * width), jnp.bfloat16),
        ),
        compiler_params=pltpu.CompilerParams(vmem_limit_bytes=44 * 1024 * 1024),
        cost_estimate=pl.CostEstimate(
            flops=4 * rows * depth * width,
            bytes_accessed=2 * rows * depth + 4 * depth * width + 10 * rows * width,
            transcendentals=rows * width,
        ),
    )(hat, weight, weight, d_hidden)


def out_weight_moves():
    moves = []
    for block in range(8 * N_Z):
        head, part = divmod(block, N_Z)
        moves.append((block, part * 2 * N_Z + head))
    return moves


def head_local(
    layer_input,
    cotangent,
    prefix,
    w_query,
    key_weight,
    value_weight,
    w_out,
    w_gate,
    w_up,
    w_down,
    attention_norm_gain,
    feedforward_norm_gain,
):
    low = jnp.bfloat16
    wide = jnp.float32
    d = lax.axis_index("dp")
    even = is_even()
    rows = w_query.shape[0]
    seq_rows = layer_input.shape[1] * 2 * N_Z
    ff_part = w_down.shape[0]
    width = 4 * ff_part
    cols = 2 * HEAD_SIZE

    def dot(left, right):
        return jnp.dot(left, right, preferred_element_type=wide)

    def dot_t(left, right):
        return lax.dot_general(left, right, (((1,), (1,)), ((), ())), preferred_element_type=wide)

    def t_dot(left, right):
        return lax.dot_general(left, right, (((0,), (0,)), ((), ())), preferred_element_type=wide)

    def lowered(weight):
        return weight.astype(low).astype(wide)

    def turned(values):
        size = values.shape[1] // 4
        return jnp.concatenate(
            [lax.dynamic_slice_in_dim(values, (d ^ e) * size, size, 1) for e in range(4)], axis=1
        )

    def block_columns(values, e):
        size = values.shape[1] // 4
        return lax.dynamic_slice_in_dim(values, e * size, size, 1)

    x_rows = layer_input[0].astype(wide)
    d_out = cotangent[0]
    gain_a = lowered(attention_norm_gain)[:, None]
    gain_m = lowered(feedforward_norm_gain)[:, None]
    low_q, low_k, low_v = lowered(w_query), lowered(key_weight), lowered(value_weight)
    low_g, low_u = lowered(w_gate), lowered(w_up)

    moves = out_weight_moves()
    out_own = lax.ppermute(w_out.astype(low), ("dp", "ctx"), moves)

    inverse1 = lax.rsqrt(jnp.mean(x_rows * x_rows, axis=-1, keepdims=True) + NORM_EPSILON)
    hat1 = x_rows * inverse1
    sent1 = turned(layer_input[0])

    q_cols = (low_q * gain_a).astype(low).reshape(rows, N_Z, 2, HEAD_SIZE).transpose(1, 2, 0, 3)
    k_cols = (low_k * gain_a).astype(low).reshape(rows, N_Z, 1, HEAD_SIZE).transpose(1, 2, 0, 3)
    v_cols = (low_v * gain_a).astype(low).reshape(rows, N_Z, 1, HEAD_SIZE).transpose(1, 2, 0, 3)
    proj_blocks = jnp.concatenate([q_cols, jnp.concatenate([k_cols, v_cols], axis=1)], axis=3)
    proj_own = exchange_ctx(proj_blocks.reshape(2 * N_Z, rows, cols))
    all_rows = gather_ctx(sent1)
    proj_own = proj_own.reshape(2 * N_Z * rows, cols)
    proj_first, proj_second = send_dp(proj_own, 1, 2), send_dp(proj_own, 2, 1)
    gain_late = after(gain_m, proj_own)

    def ff_columns(weight):
        blocks = (weight * gain_late).astype(low).reshape(rows, 4, N_Z, 2, ff_part)
        return blocks.transpose(2, 3, 0, 1, 4).reshape(N_Z, 2, rows, width)

    gate_up_blocks = jnp.concatenate([ff_columns(low_g), ff_columns(low_u)], axis=3)
    down_own = w_down.astype(low)
    all_rows, out_own, down_own, gate_up_blocks, proj_first, proj_second = (
        lax.optimization_barrier(
            (all_rows, out_own, down_own, gate_up_blocks, proj_first, proj_second)
        )
    )
    proj_third = send_dp(proj_first, 2, 1)
    all_cot = gather_ctx(after(d_out, all_rows))
    all_rows = all_rows.astype(wide)
    all_hat1 = all_rows * lax.rsqrt(
        jnp.mean(all_rows * all_rows, axis=-1, keepdims=True) + NORM_EPSILON
    )
    all_hat1 = all_hat1.astype(low)
    proj = stack_dp(proj_own, proj_first, proj_second, proj_third)
    gate_up_own = exchange_ctx(gate_up_blocks.reshape(2 * N_Z, rows, 2 * width))
    positions = jnp.arange(seq_rows, dtype=jnp.int32)
    cosine, sine = rope_angles(positions, HEAD_SIZE)
    cosine, sine = cosine[:, 0], sine[:, 0]
    half = HEAD_SIZE // 2

    def rotate(v, turn):
        a, b = v[:, :half], v[:, half:]
        return jnp.concatenate([a * cosine - turn * b * sine, b * cosine + turn * a * sine], axis=1)

    qkv = dot(all_hat1, proj)
    scale = HEAD_SIZE ** (-0.5)
    q_rot = (rotate(qkv[:, :HEAD_SIZE], 1.0) * scale).astype(low)
    own = qkv[:, HEAD_SIZE:]
    own = jnp.where(even, rotate(own, 1.0), own).astype(low)
    own, q_rot, out_own, down_own = lax.optimization_barrier((own, q_rot, out_own, down_own))
    out_first, out_second = send_dp(out_own, 1, 2), send_dp(out_own, 2, 1)
    out_w = place_dp(out_own, out_first, out_second, send_dp(out_first, 2, 1))
    down_first, down_second = send_dp(down_own, 1, 2), send_dp(down_own, 2, 1)
    other = swap_cores(own)
    keys = jnp.where(even, own, other)
    values = jnp.where(even, other, own)
    allowed = (positions[None, :] <= positions[:, None]) | (positions[None, :] < prefix[0])
    scores = jnp.where(allowed, dot_t(q_rot, keys), -1e30)
    peak = jnp.max(scores, axis=-1, keepdims=True)
    weights = jnp.exp(scores - peak)
    total = jnp.sum(weights, axis=-1, keepdims=True)
    attended = dot(weights.astype(low), values) / total
    attn = attended.astype(low)
    branch_part = dot(attn, out_w).astype(low)
    down_third = send_dp(down_first, 2, 1)
    branch_part, all_cot, down_second, down_third, gate_up_own = lax.optimization_barrier(
        (branch_part, all_cot, down_second, down_third, gate_up_own)
    )
    gate_up_own = gate_up_own.reshape(2 * N_Z * rows, 2 * width)
    branch = scatter_ctx(branch_part)
    gu_first, gu_second = send_dp(gate_up_own, 1, 2), send_dp(gate_up_own, 2, 1)
    middle = x_rows + branch

    inverse2 = lax.rsqrt(jnp.mean(middle * middle, axis=-1, keepdims=True) + NORM_EPSILON)
    hat2 = middle * inverse2
    sent2, gu_first, gu_second = lax.optimization_barrier(
        (turned(hat2).astype(low), gu_first, gu_second)
    )
    all_hat2 = gather_ctx(sent2)
    gu_third = send_dp(gu_first, 2, 1)
    gate_up_w = stack_dp(gate_up_own, gu_first, gu_second, gu_third)
    down_w = place_dp(down_own, down_first, down_second, down_third)
    d_hidden = dot_t(all_cot, down_w)
    all_hat2, gate_up_w, down_w, all_cot, d_hidden = lax.optimization_barrier(
        (all_hat2, gate_up_w, down_w, all_cot, d_hidden)
    )
    hidden, d_gate_up = feedforward(all_hat2, gate_up_w, d_hidden)
    e2_part = dot_t(d_gate_up, gate_up_w).astype(low)
    e2 = scatter_ctx(e2_part)
    d_gate_up, hidden = lax.optimization_barrier((d_gate_up, hidden, e2_part))[:2]

    def gu_block(j):
        return t_dot(block_columns(all_hat2, j), d_gate_up)

    def down_block(j):
        return t_dot(block_columns(hidden, d ^ j), all_cot)

    gu_across = send_dp(gu_block(3).astype(low), 2, 1)
    gu_far = send_dp(gu_block(3 - near_bit()).astype(low), 2, 1)
    gu_near_term, gu_own_term = gu_block(near_bit()), gu_block(0)
    z = lax.axis_index("ctx") // 2
    size = seq_rows // N_Z
    out_slots = [
        dot(lax.dynamic_slice_in_dim(hidden, (z + j) % N_Z * size, size, 0), down_w).astype(low)
        for j in range(N_Z)
    ]
    carried = sum_step(out_slots, None, 3)
    down_sent3 = down_block(3).astype(low)
    down_sent_far = down_block(3 - near_bit()).astype(low)
    gu_relay = (gu_near_term + gu_across.astype(wide)).astype(low)
    e2, gu_relay, gu_far, down_sent3, down_sent_far, carried = lax.optimization_barrier(
        (e2, gu_relay, gu_far, down_sent3, down_sent_far, carried)
    )
    gu_near = send_dp(gu_relay, 1, 2)
    gu_own_sum = gu_own_term + gu_far.astype(wide)
    down_across, down_far = send_dp(down_sent3, 2, 1), send_dp(down_sent_far, 2, 1)
    e2 = turned(e2)
    d_middle = d_out.astype(wide) + inverse2 * (
        e2 - hat2 * jnp.mean(e2 * hat2, axis=-1, keepdims=True)
    )
    branch_low = d_middle.astype(low)
    all_branch = gather_ctx(branch_low)
    carried = sum_step(out_slots, carried, 2)
    gate_up_sum = (gu_own_sum + gu_near.astype(wide)).astype(low)

    gate_up_source = gate_up_sum.reshape(2 * N_Z, rows, 2 * width)
    gate_up_sum = exchange_ctx(gate_up_source)
    all_branch, down_across = lax.optimization_barrier((all_branch, down_across, gate_up_source))[:2]

    def out_block(j):
        return lax.dynamic_slice_in_dim(head_part, (d ^ j) * rows, rows, 0)

    down_near = send_dp((down_block(near_bit()) + down_across.astype(wide)).astype(low), 1, 2)
    d_attn = dot_t(all_branch, out_w).astype(low)
    head_part = t_dot(attn, after(all_branch, d_attn))
    out_across = send_dp(out_block(3).astype(low), 2, 1)
    out_far = send_dp(out_block(3 - near_bit()).astype(low), 2, 1)
    delta = jnp.sum(d_attn.astype(wide) * attended, axis=-1, keepdims=True)
    probs = weights / total
    d_scores = (probs * (dot_t(d_attn, values) - delta)).astype(low)
    d_scores, out_across, carried, gate_up_sum = lax.optimization_barrier(
        (d_scores, out_across, carried, gate_up_sum)
    )
    carried = sum_step(out_slots, carried, 1)
    out_near = send_dp((out_block(near_bit()) + out_across.astype(wide)).astype(low), 1, 2)
    d_query = rotate(dot(d_scores, keys) * scale, -1.0)
    dk_part = t_dot(d_scores, q_rot)
    dv_part = t_dot(probs.astype(low), d_attn)
    mine = jnp.where(even, dk_part, dv_part)
    mine = mine + swap_cores(jnp.where(even, dv_part, dk_part).astype(low)).astype(wide)
    mine = jnp.where(even, rotate(mine, -1.0), mine)
    d_proj = jnp.concatenate([d_query, mine], axis=1).astype(low)
    e1_part = dot_t(d_proj, proj).astype(low)
    e1_part, out_near, down_near, carried = lax.optimization_barrier(
        (e1_part, out_near, down_near, carried)
    )
    e1 = turned(scatter_ctx(e1_part))
    d_proj = after(d_proj, e1_part)

    def proj_block(j):
        return t_dot(block_columns(all_hat1, j), d_proj)

    proj_across = send_dp(proj_block(3).astype(low), 2, 1)
    proj_far = send_dp(proj_block(3 - near_bit()).astype(low), 2, 1)
    relayed = (proj_block(near_bit()) + proj_across.astype(wide)).astype(low)
    proj_near = send_dp(relayed, 1, 2)
    out_near = after(out_near, proj_across)
    out_sum = out_block(0) + out_far.astype(wide) + out_near.astype(wide)
    out_sum = lax.ppermute(
        out_sum.astype(low), ("dp", "ctx"), [(to, start) for start, to in moves]
    )
    proj_sum = proj_block(0) + proj_far.astype(wide) + proj_near.astype(wide)
    proj_sum = proj_sum.astype(low)
    out_branch = sum_end(out_slots, after(carried, proj_sum))
    output = (middle + out_branch).astype(low)[None]
    proj_sum = exchange_ctx(proj_sum.reshape(2 * N_Z, rows, cols))
    down_sum = down_block(0) + down_far.astype(wide) + down_near.astype(wide)
    out_sum, proj_sum = lax.optimization_barrier((out_sum, proj_sum))
    out_sum = out_sum.astype(wide)

    gate_sum, up_sum, gain_mlp = finish_feedforward(gate_up_sum, w_gate, w_up, gain_m)
    gain_mlp = gain_mlp[:, 0]
    proj_sum = proj_sum.astype(wide).transpose(1, 0, 2)
    raw_q = proj_sum[:, :, :HEAD_SIZE].reshape(rows, QUERY_HEADS * HEAD_SIZE)
    kv_sum = proj_sum[:, :, HEAD_SIZE:].reshape(rows, KEY_VALUE_HEADS, 2, HEAD_SIZE)
    raw_k = kv_sum[:, :, 0].reshape(rows, KEY_VALUE_HEADS * HEAD_SIZE)
    raw_v = kv_sum[:, :, 1].reshape(rows, KEY_VALUE_HEADS * HEAD_SIZE)
    gain_attn = (
        jnp.sum(raw_q * low_q, axis=1)
        + jnp.sum(raw_k * low_k, axis=1)
        + jnp.sum(raw_v * low_v, axis=1)
    )
    d_input = d_middle + inverse1 * (e1 - hat1 * jnp.mean(e1 * hat1, axis=-1, keepdims=True))
    return (
        output,
        d_input.astype(low)[None],
        raw_q * gain_a,
        raw_k * gain_a,
        raw_v * gain_a,
        out_sum,
        gate_sum,
        up_sum,
        down_sum,
        gain_attn,
        gain_mlp,
    )


def solution(mesh):
    local = head_local if (mesh.shape["dp"], mesh.shape["ctx"]) == (4, 2 * N_Z) else gathered_local
    in_specs = (
        P("dp", "ctx", None),
        P("dp", "ctx", None),
        P("dp"),
        P(("dp", "ctx"), None),
        P(("dp", "ctx"), None),
        P(("dp", "ctx"), None),
        P(("dp", "ctx"), None),
        P(("dp", "ctx"), None),
        P(("dp", "ctx"), None),
        P(("dp", "ctx"), None),
        P(("dp", "ctx")),
        P(("dp", "ctx")),
    )
    out_specs = (
        P("dp", "ctx", None),
        P("dp", "ctx", None),
        P(("dp", "ctx"), None),
        P(("dp", "ctx"), None),
        P(("dp", "ctx"), None),
        P(("dp", "ctx"), None),
        P(("dp", "ctx"), None),
        P(("dp", "ctx"), None),
        P(("dp", "ctx"), None),
        P(("dp", "ctx")),
        P(("dp", "ctx")),
    )
    return jax.shard_map(local, mesh=mesh, in_specs=in_specs, out_specs=out_specs, check_vma=False)
```

```python
import jax
import jax.numpy as jnp
from jax import lax
from jax.experimental import pallas as pl
from jax.experimental.pallas import tpu as pltpu
from jax.sharding import PartitionSpec as P

FF = 8192
QUERY_HEADS = 8
KEY_VALUE_HEADS = 4
HEAD_SIZE = 256


NORM_EPSILON = 1e-06
THETA = 1000042.0


def rope_angles(token_positions, width):
    half_width = width // 2
    frequency = jnp.power(THETA, -(2.0 * jnp.arange(half_width, dtype=jnp.float32) / width))
    angles = token_positions.astype(jnp.float32)[:, None] * frequency[None, :]
    return (jnp.cos(angles)[:, None, :], jnp.sin(angles)[:, None, :])


def apply_rotary(vector, cosine_table, sines_lookup):
    half_width = vector.shape[-1] // 2
    first_half = vector[..., :half_width]
    second_half = vector[..., half_width:]
    return jnp.concatenate(
        [
            first_half * cosine_table - second_half * sines_lookup,
            second_half * cosine_table + first_half * sines_lookup,
        ],
        axis=-1,
    )


def reverse_rotary(vector, cosine_table, sines_lookup):
    half_width = vector.shape[-1] // 2
    first_half = vector[..., :half_width]
    second_half = vector[..., half_width:]
    return jnp.concatenate(
        [
            first_half * cosine_table + second_half * sines_lookup,
            second_half * cosine_table - first_half * sines_lookup,
        ],
        axis=-1,
    )


def norm_backward(d_normed, hat_values, gain_row, inverse):
    scaled = d_normed * gain_row
    return inverse * (scaled - hat_values * jnp.mean(scaled * hat_values, axis=-1, keepdims=True))


def column_product(left, right):
    return jnp.einsum("bd,bf->df", left, right, preferred_element_type=jnp.float32)


def gathered_local(
    layer_input,
    cotangent,
    prefix,
    w_query,
    key_weight,
    value_weight,
    w_out,
    w_gate,
    w_up,
    w_down,
    attention_norm_gain,
    feedforward_norm_gain,
):
    narrow_number_type = jnp.bfloat16
    wide_number_type = jnp.float32
    token_rows = layer_input.shape[1]
    query_group_width = QUERY_HEADS // KEY_VALUE_HEADS
    attention_score_scale = HEAD_SIZE ** (-0.5)
    input_rows_all = layer_input[0].astype(wide_number_type)
    first_row = lax.axis_index("ctx") * token_rows
    token_positions = first_row + jnp.arange(token_rows, dtype=jnp.int32)
    prefix_len = prefix[0]
    cosine_table, sines_lookup = rope_angles(token_positions, HEAD_SIZE)
    attn_kept = (
        lax.all_gather(w_query.astype(narrow_number_type), ("dp", "ctx"), axis=0, tiled=True),
        lax.all_gather(key_weight.astype(narrow_number_type), ("dp", "ctx"), axis=0, tiled=True),
        lax.all_gather(value_weight.astype(narrow_number_type), ("dp", "ctx"), axis=0, tiled=True),
        lax.all_gather(w_out.astype(narrow_number_type), ("dp", "ctx"), axis=0, tiled=True),
        lax.all_gather(
            attention_norm_gain.astype(narrow_number_type), ("dp", "ctx"), axis=0, tiled=True
        ),
    )
    query_w, key_matrix, value_w, out_w, attention_gain = attn_kept
    first_inverse_norm = lax.rsqrt(
        jnp.mean(input_rows_all * input_rows_all, axis=-1, keepdims=True) + NORM_EPSILON
    )
    first_standardized = input_rows_all * first_inverse_norm
    first_normalized = (first_standardized * attention_gain.astype(wide_number_type)).astype(
        narrow_number_type
    )
    query_rows = jnp.dot(
        first_normalized, query_w, preferred_element_type=wide_number_type
    ).reshape(token_rows, QUERY_HEADS, HEAD_SIZE)
    projected_keys = jnp.dot(
        first_normalized, key_matrix, preferred_element_type=wide_number_type
    ).reshape(token_rows, KEY_VALUE_HEADS, HEAD_SIZE)
    value_rows = jnp.dot(first_normalized, value_w, preferred_element_type=wide_number_type).astype(
        narrow_number_type
    )
    rotated_queries = apply_rotary(query_rows, cosine_table, sines_lookup).astype(
        narrow_number_type
    )
    rotated_keys = (
        apply_rotary(projected_keys, cosine_table, sines_lookup)
        .astype(narrow_number_type)
        .reshape(token_rows, KEY_VALUE_HEADS * HEAD_SIZE)
    )
    grouped_queries = rotated_queries.reshape(
        token_rows, KEY_VALUE_HEADS, query_group_width, HEAD_SIZE
    )

    def masked_scores(key_segment, start_row):
        segment_rows = key_segment.shape[0]
        columns = start_row + jnp.arange(segment_rows, dtype=jnp.int32)
        allowed = (columns[None, :] <= token_positions[:, None]) | (columns[None, :] < prefix_len)
        scores = (
            jnp.einsum(
                "bkgd,jkd->kgbj",
                grouped_queries,
                key_segment.reshape(segment_rows, KEY_VALUE_HEADS, HEAD_SIZE),
                preferred_element_type=wide_number_type,
            )
            * attention_score_scale
        )
        return jnp.where(allowed[None, None], scores, -jnp.inf)

    row_maximum = jnp.full(
        (KEY_VALUE_HEADS, query_group_width, token_rows), -1e30, wide_number_type
    )
    key_segment = lax.all_gather(rotated_keys, "ctx", axis=0, tiled=True)
    value_segment = lax.all_gather(value_rows, "ctx", axis=0, tiled=True)
    segment_rows = value_segment.shape[0]
    scores = masked_scores(key_segment, jnp.int32(0))
    new_peak = jnp.maximum(row_maximum, jnp.max(scores, axis=-1))
    soft_part = jnp.exp(scores - new_peak[..., None])
    row_denominator = jnp.sum(soft_part, axis=-1)
    weighted_values = jnp.einsum(
        "kgbj,jkd->bkgd",
        soft_part.astype(narrow_number_type),
        value_segment.reshape(segment_rows, KEY_VALUE_HEADS, HEAD_SIZE),
        preferred_element_type=wide_number_type,
    )
    row_maximum, row_denominator, weighted_values = (new_peak, row_denominator, weighted_values)
    log_total = row_maximum + jnp.log(row_denominator)
    attention_result = weighted_values / jnp.transpose(row_denominator, (2, 0, 1))[..., None]
    attn_out = attention_result.reshape(token_rows, QUERY_HEADS * HEAD_SIZE).astype(
        narrow_number_type
    )
    hidden_middle = input_rows_all + jnp.dot(
        attn_out, out_w, preferred_element_type=wide_number_type
    )
    mlp_kept = (
        lax.all_gather(w_gate.astype(narrow_number_type), ("dp", "ctx"), axis=0, tiled=True),
        lax.all_gather(w_up.astype(narrow_number_type), ("dp", "ctx"), axis=0, tiled=True),
        lax.all_gather(w_down.astype(narrow_number_type), ("dp", "ctx"), axis=0, tiled=True),
        lax.all_gather(
            feedforward_norm_gain.astype(narrow_number_type), ("dp", "ctx"), axis=0, tiled=True
        ),
    )
    gate_w, up_w, down_w, feedforward_gain = mlp_kept
    second_inverse_norm = lax.rsqrt(
        jnp.mean(hidden_middle * hidden_middle, axis=-1, keepdims=True) + NORM_EPSILON
    )
    second_standardized = hidden_middle * second_inverse_norm
    second_normalized = (second_standardized * feedforward_gain.astype(wide_number_type)).astype(
        narrow_number_type
    )
    gate_proj = jnp.dot(second_normalized, gate_w, preferred_element_type=wide_number_type)
    up_proj = jnp.dot(second_normalized, up_w, preferred_element_type=wide_number_type)
    hidden = (jax.nn.silu(gate_proj) * up_proj).astype(narrow_number_type)
    result = hidden_middle + jnp.dot(hidden, down_w, preferred_element_type=wide_number_type)
    output = result.astype(narrow_number_type)[None]
    gate_w, up_w, down_w, feedforward_gain = (
        lax.all_gather(w_gate.astype(narrow_number_type), ("dp", "ctx"), axis=0, tiled=True),
        lax.all_gather(w_up.astype(narrow_number_type), ("dp", "ctx"), axis=0, tiled=True),
        lax.all_gather(w_down.astype(narrow_number_type), ("dp", "ctx"), axis=0, tiled=True),
        lax.all_gather(
            feedforward_norm_gain.astype(narrow_number_type), ("dp", "ctx"), axis=0, tiled=True
        ),
    )
    d_out = cotangent[0]
    down_sum = lax.psum_scatter(
        column_product(hidden, d_out), ("dp", "ctx"), scatter_dimension=0, tiled=True
    )
    d_hidden = jnp.einsum("bd,fd->bf", d_out, down_w, preferred_element_type=wide_number_type)
    sigmoid_gate = jax.nn.sigmoid(gate_proj)
    d_gate = (d_hidden * up_proj * sigmoid_gate * (1.0 + gate_proj * (1.0 - sigmoid_gate))).astype(
        narrow_number_type
    )
    d_up = (d_hidden * gate_proj * sigmoid_gate).astype(narrow_number_type)
    second_normalized_gradient = jnp.einsum(
        "bf,df->bd", d_gate, gate_w, preferred_element_type=wide_number_type
    ) + jnp.einsum("bf,df->bd", d_up, up_w, preferred_element_type=wide_number_type)
    gate_and_up = jnp.concatenate([d_gate, d_up], axis=1)
    both_sum = lax.psum_scatter(
        column_product(second_normalized, gate_and_up),
        ("dp", "ctx"),
        scatter_dimension=0,
        tiled=True,
    )
    gate_sum = both_sum[:, :FF]
    up_sum = both_sum[:, FF:]
    feedforward_gain_part = jnp.sum(second_normalized_gradient * second_standardized, axis=0)
    middle_gradient = d_out.astype(wide_number_type) + norm_backward(
        second_normalized_gradient,
        second_standardized,
        feedforward_gain.astype(wide_number_type),
        second_inverse_norm,
    )
    query_w, key_matrix, value_w, out_w, attention_gain = (
        lax.all_gather(w_query.astype(narrow_number_type), ("dp", "ctx"), axis=0, tiled=True),
        lax.all_gather(key_weight.astype(narrow_number_type), ("dp", "ctx"), axis=0, tiled=True),
        lax.all_gather(value_weight.astype(narrow_number_type), ("dp", "ctx"), axis=0, tiled=True),
        lax.all_gather(w_out.astype(narrow_number_type), ("dp", "ctx"), axis=0, tiled=True),
        lax.all_gather(
            attention_norm_gain.astype(narrow_number_type), ("dp", "ctx"), axis=0, tiled=True
        ),
    )
    d_branch = middle_gradient.astype(narrow_number_type)
    out_sum = lax.psum_scatter(
        column_product(attn_out, d_branch), ("dp", "ctx"), scatter_dimension=0, tiled=True
    )
    attention_gradient = jnp.einsum(
        "bd,hd->bh", d_branch, out_w, preferred_element_type=wide_number_type
    ).astype(narrow_number_type)
    attention_group_gradient = attention_gradient.reshape(
        token_rows, KEY_VALUE_HEADS, query_group_width, HEAD_SIZE
    )
    delta_rows = jnp.transpose(
        jnp.sum(attention_group_gradient.astype(wide_number_type) * attention_result, axis=-1),
        (1, 2, 0),
    )
    gathered_keys, gathered_values = (
        lax.all_gather(rotated_keys, "ctx", axis=0, tiled=True),
        lax.all_gather(value_rows, "ctx", axis=0, tiled=True),
    )
    count_of_blocks = gathered_keys.shape[0] // token_rows
    stacked_key_blocks = gathered_keys.reshape(
        count_of_blocks, token_rows, KEY_VALUE_HEADS * HEAD_SIZE
    )
    stacked_value_blocks = gathered_values.reshape(
        count_of_blocks, token_rows, KEY_VALUE_HEADS, HEAD_SIZE
    )

    def back_step(d_query_sum, block_item):
        current_key_block, value_block, block_index = block_item
        scores = masked_scores(current_key_block, block_index * token_rows)
        soft_part = jnp.exp(scores - log_total[..., None])
        d_value_block = jnp.einsum(
            "kgbj,bkgd->jkd",
            soft_part.astype(narrow_number_type),
            attention_group_gradient,
            preferred_element_type=wide_number_type,
        )
        d_probs = jnp.einsum(
            "bkgd,jkd->kgbj",
            attention_group_gradient,
            value_block,
            preferred_element_type=wide_number_type,
        )
        d_scores = (soft_part * (d_probs - delta_rows[..., None])).astype(narrow_number_type)
        key_tensor_triple = current_key_block.reshape(token_rows, KEY_VALUE_HEADS, HEAD_SIZE)
        d_query_sum = d_query_sum + jnp.einsum(
            "kgbj,jkd->bkgd", d_scores, key_tensor_triple, preferred_element_type=wide_number_type
        )
        d_key_block = jnp.einsum(
            "kgbj,bkgd->jkd", d_scores, grouped_queries, preferred_element_type=wide_number_type
        )
        return (d_query_sum, (d_key_block, d_value_block))

    d_query_sum, (key_gradients, value_gradients) = lax.scan(
        back_step,
        jnp.zeros((token_rows, KEY_VALUE_HEADS, query_group_width, HEAD_SIZE), wide_number_type),
        (stacked_key_blocks, stacked_value_blocks, jnp.arange(count_of_blocks, dtype=jnp.int32)),
    )
    key_gradients = (
        key_gradients.reshape(count_of_blocks * token_rows, KEY_VALUE_HEADS * HEAD_SIZE)
        * attention_score_scale
    )
    value_gradients = value_gradients.reshape(
        count_of_blocks * token_rows, KEY_VALUE_HEADS * HEAD_SIZE
    )
    local_keys, own_values = (
        lax.psum_scatter(
            key_gradients.astype(jnp.bfloat16), "ctx", scatter_dimension=0, tiled=True
        ).astype(jnp.float32),
        lax.psum_scatter(
            value_gradients.astype(jnp.bfloat16), "ctx", scatter_dimension=0, tiled=True
        ).astype(jnp.float32),
    )
    d_key = (
        reverse_rotary(
            local_keys.reshape(token_rows, KEY_VALUE_HEADS, HEAD_SIZE), cosine_table, sines_lookup
        )
        .reshape(token_rows, KEY_VALUE_HEADS * HEAD_SIZE)
        .astype(narrow_number_type)
    )
    d_value = own_values.astype(narrow_number_type)
    d_query = reverse_rotary(
        (d_query_sum * attention_score_scale).reshape(token_rows, QUERY_HEADS, HEAD_SIZE),
        cosine_table,
        sines_lookup,
    )
    d_query = d_query.reshape(token_rows, QUERY_HEADS * HEAD_SIZE).astype(narrow_number_type)
    d_projected = jnp.concatenate([d_query, d_key, d_value], axis=1)
    projection_total = lax.psum_scatter(
        column_product(first_normalized, d_projected),
        ("dp", "ctx"),
        scatter_dimension=0,
        tiled=True,
    )
    query_sum = projection_total[:, : QUERY_HEADS * HEAD_SIZE]
    key_gradient_sum = projection_total[
        :, QUERY_HEADS * HEAD_SIZE : QUERY_HEADS * HEAD_SIZE + KEY_VALUE_HEADS * HEAD_SIZE
    ]
    value_gradient_sum = projection_total[
        :, QUERY_HEADS * HEAD_SIZE + KEY_VALUE_HEADS * HEAD_SIZE :
    ]
    first_normalized_gradient = (
        jnp.einsum("bh,dh->bd", d_query, query_w, preferred_element_type=wide_number_type)
        + jnp.einsum("bh,dh->bd", d_key, key_matrix, preferred_element_type=wide_number_type)
        + jnp.einsum("bh,dh->bd", d_value, value_w, preferred_element_type=wide_number_type)
    )
    attention_gain_part = jnp.sum(first_normalized_gradient * first_standardized, axis=0)
    gradient_of_input = middle_gradient + norm_backward(
        first_normalized_gradient,
        first_standardized,
        attention_gain.astype(wide_number_type),
        first_inverse_norm,
    )
    attn_gain_sum, mlp_gain_sum = (
        lax.psum_scatter(attention_gain_part, ("dp", "ctx"), scatter_dimension=0, tiled=True),
        lax.psum_scatter(feedforward_gain_part, ("dp", "ctx"), scatter_dimension=0, tiled=True),
    )
    input_grad = gradient_of_input.astype(narrow_number_type)[None]
    return (
        output,
        input_grad,
        query_sum,
        key_gradient_sum,
        value_gradient_sum,
        out_sum,
        gate_sum,
        up_sum,
        down_sum,
        attn_gain_sum,
        mlp_gain_sum,
    )

N_Z = 4


def after(value, *others):
    return lax.optimization_barrier((value,) + others)[0]


def swap_cores(values):
    return lax.ppermute(values, "ctx", [(i, i ^ 1) for i in range(2 * N_Z)])


def gather_ctx(rows):
    return lax.all_gather(rows, "ctx", axis=0, tiled=True)


def scatter_ctx(partial):
    return lax.psum_scatter(partial, "ctx", scatter_dimension=0, tiled=True).astype(jnp.float32)


def hop(values, lowest, highest):
    moves = [(2 * z, 2 * z + 2) for z in range(lowest, highest + 1)]
    moves += [(2 * (N_Z - 1 - z) + 1, 2 * (N_Z - 1 - z) - 1) for z in range(lowest, highest + 1)]
    return lax.ppermute(values, "ctx", moves)


def sum_step(slots, carried, step):
    low, wide = jnp.bfloat16, jnp.float32
    keep = jnp.where(is_even(), slots[step], slots[N_Z - step])
    give = jnp.where(is_even(), slots[N_Z - step], slots[step])
    total = keep.astype(wide) + swap_cores(give).astype(wide)
    if carried is not None:
        total = total + carried.astype(wide)
    return hop(total.astype(low), 0, N_Z - 1 - step)


def sum_end(slots, carried):
    low, wide = jnp.bfloat16, jnp.float32
    total = slots[0].astype(wide) + carried.astype(wide)
    half = total.shape[0] // 2
    give = jnp.where(is_even(), total[half:], total[:half]).astype(low)
    return jnp.where(is_even(), total[:half], total[half:]) + swap_cores(give).astype(wide)


def send_dp(values, first, second):
    moves = [(d, c, d ^ (second if c % 2 else first)) for d in range(4) for c in range(2 * N_Z)]
    moves = [(d * 2 * N_Z + c, to * 2 * N_Z + c) for d, c, to in moves]
    return lax.ppermute(values, ("dp", "ctx"), moves)


def is_even():
    return lax.axis_index("ctx") % 2 == 0


def near_bit():
    return jnp.where(is_even(), 1, 2)


def place_dp(rows, first, second, third):
    d = lax.axis_index("dp")
    size = rows.shape[0]
    whole = jnp.zeros((4 * size,) + rows.shape[1:], rows.dtype)
    for block, place in (
        (rows, d),
        (first, d ^ near_bit()),
        (second, d ^ (3 - near_bit())),
        (third, d ^ 3),
    ):
        whole = lax.dynamic_update_slice_in_dim(whole, block, place * size, 0)
    return whole


def stack_dp(rows, first, second, third):
    one = jnp.where(is_even(), first, second)
    two = jnp.where(is_even(), second, first)
    return jnp.concatenate([rows, one, two, third], axis=0)


def exchange_ctx(blocks):
    return lax.all_to_all(blocks, "ctx", 0, 0, tiled=True)


def finish_feedforward(sums, w_gate, w_up, gain):
    n_ctx, rows, both = sums.shape
    part = both // 8

    def kernel(sums_ref, gate_ref, up_ref, gain_ref, gate_out, up_out, gain_out):
        scale = gain_ref[...]
        total = jnp.zeros((rows, part), jnp.float32)
        for d in range(4):
            for c in range(n_ctx):
                place = pl.ds((d * n_ctx + c) * part, part)
                for half, weight_ref, out_ref in ((0, gate_ref, gate_out), (1, up_ref, up_out)):
                    raw = sums_ref[c, :, pl.ds((half * 4 + d) * part, part)].astype(jnp.float32)
                    weight = weight_ref[:, place].astype(jnp.bfloat16).astype(jnp.float32)
                    total = total + raw * weight
                    out_ref[:, place] = raw * scale
        gain_out[...] = jnp.sum(total, axis=1, keepdims=True)

    return pl.pallas_call(
        kernel,
        out_shape=(
            jax.ShapeDtypeStruct(w_gate.shape, jnp.float32),
            jax.ShapeDtypeStruct(w_up.shape, jnp.float32),
            jax.ShapeDtypeStruct((rows, 1), jnp.float32),
        ),
        compiler_params=pltpu.CompilerParams(vmem_limit_bytes=32 * 1024 * 1024),
        cost_estimate=pl.CostEstimate(
            flops=4 * w_gate.size, bytes_accessed=20 * w_gate.size, transcendentals=0
        ),
    )(sums, w_gate, w_up, gain)


def feedforward(hat, weight, d_hidden):
    rows, depth = hat.shape
    width = weight.shape[1] // 2
    tile, chunk = 256, 256
    tiles = width // tile

    def kernel(hat_ref, gate_ref, up_ref, grad_ref, hidden_ref, out_ref):
        place = pl.multiple_of(pl.program_id(0) * tile, tile)
        for start in range(0, rows, chunk):
            part = pl.ds(start, chunk)
            left = hat_ref[part, :]
            gate = jnp.dot(left, gate_ref[...], preferred_element_type=jnp.float32)
            up = jnp.dot(left, up_ref[...], preferred_element_type=jnp.float32)
            sig = jax.nn.sigmoid(gate)
            silu = gate * sig
            grad = grad_ref[part, :]
            hidden_ref[part, :] = (silu * up).astype(jnp.bfloat16)
            d_gate = grad * up * sig * (1.0 + gate * (1.0 - sig))
            out_ref[part, pl.ds(place, tile)] = d_gate.astype(jnp.bfloat16)
            out_ref[part, pl.ds(width + place, tile)] = (grad * silu).astype(jnp.bfloat16)

    return pl.pallas_call(
        kernel,
        grid=(tiles,),
        in_specs=[
            pl.BlockSpec((rows, depth), lambda j: (0, 0)),
            pl.BlockSpec((depth, tile), lambda j: (0, j)),
            pl.BlockSpec((depth, tile), lambda j: (0, tiles + j)),
            pl.BlockSpec((rows, tile), lambda j: (0, j)),
        ],
        out_specs=(
            pl.BlockSpec((rows, tile), lambda j: (0, j)),
            pl.BlockSpec((rows, 2 * width), lambda j: (0, 0)),
        ),
        out_shape=(
            jax.ShapeDtypeStruct((rows, width), jnp.bfloat16),
            jax.ShapeDtypeStruct((rows, 2 * width), jnp.bfloat16),
        ),
        compiler_params=pltpu.CompilerParams(vmem_limit_bytes=44 * 1024 * 1024),
        cost_estimate=pl.CostEstimate(
            flops=4 * rows * depth * width,
            bytes_accessed=2 * rows * depth + 4 * depth * width + 10 * rows * width,
            transcendentals=rows * width,
        ),
    )(hat, weight, weight, d_hidden)


def out_weight_moves():
    moves = []
    for block in range(8 * N_Z):
        head, part = divmod(block, N_Z)
        moves.append((block, part * 2 * N_Z + head))
    return moves


def head_local(
    layer_input,
    cotangent,
    prefix,
    w_query,
    key_weight,
    value_weight,
    w_out,
    w_gate,
    w_up,
    w_down,
    attention_norm_gain,
    feedforward_norm_gain,
):
    low = jnp.bfloat16
    wide = jnp.float32
    d = lax.axis_index("dp")
    even = is_even()
    rows = w_query.shape[0]
    seq_rows = layer_input.shape[1] * 2 * N_Z
    ff_part = w_down.shape[0]
    width = 4 * ff_part
    cols = 2 * HEAD_SIZE

    def dot(left, right):
        return jnp.dot(left, right, preferred_element_type=wide)

    def dot_t(left, right):
        return lax.dot_general(left, right, (((1,), (1,)), ((), ())), preferred_element_type=wide)

    def t_dot(left, right):
        return lax.dot_general(left, right, (((0,), (0,)), ((), ())), preferred_element_type=wide)

    def lowered(weight):
        return weight.astype(low).astype(wide)

    def turned(values):
        size = values.shape[1] // 4
        return jnp.concatenate(
            [lax.dynamic_slice_in_dim(values, (d ^ e) * size, size, 1) for e in range(4)], axis=1
        )

    def block_columns(values, e):
        size = values.shape[1] // 4
        return lax.dynamic_slice_in_dim(values, e * size, size, 1)

    x_rows = layer_input[0].astype(wide)
    d_out = cotangent[0]
    gain_a = lowered(attention_norm_gain)[:, None]
    gain_m = lowered(feedforward_norm_gain)[:, None]
    low_q, low_k, low_v = lowered(w_query), lowered(key_weight), lowered(value_weight)
    low_g, low_u = lowered(w_gate), lowered(w_up)

    moves = out_weight_moves()
    out_own = lax.ppermute(w_out.astype(low), ("dp", "ctx"), moves)

    inverse1 = lax.rsqrt(jnp.mean(x_rows * x_rows, axis=-1, keepdims=True) + NORM_EPSILON)
    hat1 = x_rows * inverse1
    sent1 = turned(layer_input[0])

    q_cols = (low_q * gain_a).astype(low).reshape(rows, N_Z, 2, HEAD_SIZE).transpose(1, 2, 0, 3)
    k_cols = (low_k * gain_a).astype(low).reshape(rows, N_Z, 1, HEAD_SIZE).transpose(1, 2, 0, 3)
    v_cols = (low_v * gain_a).astype(low).reshape(rows, N_Z, 1, HEAD_SIZE).transpose(1, 2, 0, 3)
    proj_blocks = jnp.concatenate([q_cols, jnp.concatenate([k_cols, v_cols], axis=1)], axis=3)
    proj_own = exchange_ctx(proj_blocks.reshape(2 * N_Z, rows, cols))
    all_rows = gather_ctx(sent1)
    proj_own = proj_own.reshape(2 * N_Z * rows, cols)
    proj_first, proj_second = send_dp(proj_own, 1, 2), send_dp(proj_own, 2, 1)
    gain_late = after(gain_m, proj_own)

    def ff_columns(weight):
        blocks = (weight * gain_late).astype(low).reshape(rows, 4, N_Z, 2, ff_part)
        return blocks.transpose(2, 3, 0, 1, 4).reshape(N_Z, 2, rows, width)

    gate_up_blocks = jnp.concatenate([ff_columns(low_g), ff_columns(low_u)], axis=3)
    down_own = w_down.astype(low)
    all_rows, out_own, down_own, gate_up_blocks, proj_first, proj_second = (
        lax.optimization_barrier(
            (all_rows, out_own, down_own, gate_up_blocks, proj_first, proj_second)
        )
    )
    proj_third = send_dp(proj_first, 2, 1)
    all_cot = gather_ctx(after(d_out, all_rows))
    all_rows = all_rows.astype(wide)
    all_hat1 = all_rows * lax.rsqrt(
        jnp.mean(all_rows * all_rows, axis=-1, keepdims=True) + NORM_EPSILON
    )
    all_hat1 = all_hat1.astype(low)
    proj = stack_dp(proj_own, proj_first, proj_second, proj_third)
    gate_up_own = exchange_ctx(gate_up_blocks.reshape(2 * N_Z, rows, 2 * width))
    positions = jnp.arange(seq_rows, dtype=jnp.int32)
    cosine, sine = rope_angles(positions, HEAD_SIZE)
    cosine, sine = cosine[:, 0], sine[:, 0]
    half = HEAD_SIZE // 2

    def rotate(v, turn):
        a, b = v[:, :half], v[:, half:]
        return jnp.concatenate([a * cosine - turn * b * sine, b * cosine + turn * a * sine], axis=1)

    qkv = dot(all_hat1, proj)
    scale = HEAD_SIZE ** (-0.5)
    q_rot = (rotate(qkv[:, :HEAD_SIZE], 1.0) * scale).astype(low)
    own = qkv[:, HEAD_SIZE:]
    own = jnp.where(even, rotate(own, 1.0), own).astype(low)
    own, q_rot, out_own, down_own = lax.optimization_barrier((own, q_rot, out_own, down_own))
    out_first, out_second = send_dp(out_own, 1, 2), send_dp(out_own, 2, 1)
    out_w = place_dp(out_own, out_first, out_second, send_dp(out_first, 2, 1))
    down_first, down_second = send_dp(down_own, 1, 2), send_dp(down_own, 2, 1)
    other = swap_cores(own)
    keys = jnp.where(even, own, other)
    values = jnp.where(even, other, own)
    allowed = (positions[None, :] <= positions[:, None]) | (positions[None, :] < prefix[0])
    scores = jnp.where(allowed, dot_t(q_rot, keys), -1e30)
    peak = jnp.max(scores, axis=-1, keepdims=True)
    weights = jnp.exp(scores - peak)
    total = jnp.sum(weights, axis=-1, keepdims=True)
    attended = dot(weights.astype(low), values) / total
    attn = attended.astype(low)
    branch_part = dot(attn, out_w).astype(low)
    down_third = send_dp(down_first, 2, 1)
    branch_part, all_cot, down_second, down_third, gate_up_own = lax.optimization_barrier(
        (branch_part, all_cot, down_second, down_third, gate_up_own)
    )
    gate_up_own = gate_up_own.reshape(2 * N_Z * rows, 2 * width)
    branch = scatter_ctx(branch_part)
    gu_first, gu_second = send_dp(gate_up_own, 1, 2), send_dp(gate_up_own, 2, 1)
    middle = x_rows + branch

    inverse2 = lax.rsqrt(jnp.mean(middle * middle, axis=-1, keepdims=True) + NORM_EPSILON)
    hat2 = middle * inverse2
    sent2, gu_first, gu_second = lax.optimization_barrier(
        (turned(hat2).astype(low), gu_first, gu_second)
    )
    all_hat2 = gather_ctx(sent2)
    gu_third = send_dp(gu_first, 2, 1)
    gate_up_w = stack_dp(gate_up_own, gu_first, gu_second, gu_third)
    down_w = place_dp(down_own, down_first, down_second, down_third)
    d_hidden = dot_t(all_cot, down_w)
    all_hat2, gate_up_w, down_w, all_cot, d_hidden = lax.optimization_barrier(
        (all_hat2, gate_up_w, down_w, all_cot, d_hidden)
    )
    hidden, d_gate_up = feedforward(all_hat2, gate_up_w, d_hidden)
    e2_part = dot_t(d_gate_up, gate_up_w).astype(low)
    e2 = scatter_ctx(e2_part)
    d_gate_up, hidden = lax.optimization_barrier((d_gate_up, hidden, e2_part))[:2]

    def gu_block(j):
        return t_dot(block_columns(all_hat2, j), d_gate_up)

    def down_block(j):
        return t_dot(block_columns(hidden, d ^ j), all_cot)

    gu_across = send_dp(gu_block(3).astype(low), 2, 1)
    gu_far = send_dp(gu_block(3 - near_bit()).astype(low), 2, 1)
    gu_near_term, gu_own_term = gu_block(near_bit()), gu_block(0)
    z = lax.axis_index("ctx") // 2
    size = seq_rows // N_Z
    out_slots = [
        dot(lax.dynamic_slice_in_dim(hidden, (z + j) % N_Z * size, size, 0), down_w).astype(low)
        for j in range(N_Z)
    ]
    carried = sum_step(out_slots, None, 3)
    down_sent3 = down_block(3).astype(low)
    down_sent_far = down_block(3 - near_bit()).astype(low)
    gu_relay = (gu_near_term + gu_across.astype(wide)).astype(low)
    e2, gu_relay, gu_far, down_sent3, down_sent_far, carried = lax.optimization_barrier(
        (e2, gu_relay, gu_far, down_sent3, down_sent_far, carried)
    )
    gu_near = send_dp(gu_relay, 1, 2)
    gu_own_sum = gu_own_term + gu_far.astype(wide)
    down_across, down_far = send_dp(down_sent3, 2, 1), send_dp(down_sent_far, 2, 1)
    e2 = turned(e2)
    d_middle = d_out.astype(wide) + inverse2 * (
        e2 - hat2 * jnp.mean(e2 * hat2, axis=-1, keepdims=True)
    )
    branch_low = d_middle.astype(low)
    all_branch = gather_ctx(branch_low)
    carried = sum_step(out_slots, carried, 2)
    gate_up_sum = (gu_own_sum + gu_near.astype(wide)).astype(low)

    gate_up_source = gate_up_sum.reshape(2 * N_Z, rows, 2 * width)
    gate_up_sum = exchange_ctx(gate_up_source)
    all_branch, down_across = lax.optimization_barrier((all_branch, down_across, gate_up_source))[:2]

    def out_block(j):
        return lax.dynamic_slice_in_dim(head_part, (d ^ j) * rows, rows, 0)

    down_near = send_dp((down_block(near_bit()) + down_across.astype(wide)).astype(low), 1, 2)
    d_attn = dot_t(all_branch, out_w).astype(low)
    head_part = t_dot(attn, after(all_branch, d_attn))
    out_across = send_dp(out_block(3).astype(low), 2, 1)
    out_far = send_dp(out_block(3 - near_bit()).astype(low), 2, 1)
    delta = jnp.sum(d_attn.astype(wide) * attended, axis=-1, keepdims=True)
    probs = weights / total
    d_scores = (probs * (dot_t(d_attn, values) - delta)).astype(low)
    d_scores, out_across, carried = lax.optimization_barrier((d_scores, out_across, carried))
    out_near = send_dp((out_block(near_bit()) + out_across.astype(wide)).astype(low), 1, 2)
    d_query = rotate(dot(d_scores, keys) * scale, -1.0)
    dk_part = t_dot(d_scores, q_rot)
    dv_part = t_dot(probs.astype(low), d_attn)
    mine = jnp.where(even, dk_part, dv_part)
    mine = mine + swap_cores(jnp.where(even, dv_part, dk_part).astype(low)).astype(wide)
    mine = jnp.where(even, rotate(mine, -1.0), mine)
    d_proj = jnp.concatenate([d_query, mine], axis=1).astype(low)
    e1_part = dot_t(d_proj, proj).astype(low)
    e1_part, out_near, down_near, carried = lax.optimization_barrier(
        (e1_part, out_near, down_near, carried)
    )
    e1 = turned(scatter_ctx(e1_part))
    d_proj, gate_up_sum = lax.optimization_barrier((d_proj, gate_up_sum, e1_part))[:2]

    def proj_block(j):
        return t_dot(block_columns(all_hat1, j), d_proj)

    proj_across = send_dp(proj_block(3).astype(low), 2, 1)
    proj_far = send_dp(proj_block(3 - near_bit()).astype(low), 2, 1)
    relayed = (proj_block(near_bit()) + proj_across.astype(wide)).astype(low)
    proj_near = send_dp(relayed, 1, 2)
    proj_sum = proj_block(0) + proj_far.astype(wide) + proj_near.astype(wide)
    proj_source = proj_sum.astype(low).reshape(2 * N_Z, rows, cols)
    proj_sum = exchange_ctx(proj_source)
    gate_up_sum, down_near, out_near, carried = lax.optimization_barrier(
        (gate_up_sum, down_near, out_near, carried, proj_source)
    )[:4]
    carried = sum_step(out_slots, carried, 1)
    out_sum = out_block(0) + out_far.astype(wide) + out_near.astype(wide)
    out_sum = lax.ppermute(
        out_sum.astype(low), ("dp", "ctx"), [(to, start) for start, to in moves]
    )
    out_branch = sum_end(out_slots, carried)
    output = (middle + out_branch).astype(low)[None]
    down_sum = down_block(0) + down_far.astype(wide) + down_near.astype(wide)
    out_sum, proj_sum = lax.optimization_barrier((out_sum, proj_sum))
    out_sum = out_sum.astype(wide)

    gate_sum, up_sum, gain_mlp = finish_feedforward(gate_up_sum, w_gate, w_up, gain_m)
    gain_mlp = gain_mlp[:, 0]
    proj_sum = proj_sum.astype(wide).transpose(1, 0, 2)
    raw_q = proj_sum[:, :, :HEAD_SIZE].reshape(rows, QUERY_HEADS * HEAD_SIZE)
    kv_sum = proj_sum[:, :, HEAD_SIZE:].reshape(rows, KEY_VALUE_HEADS, 2, HEAD_SIZE)
    raw_k = kv_sum[:, :, 0].reshape(rows, KEY_VALUE_HEADS * HEAD_SIZE)
    raw_v = kv_sum[:, :, 1].reshape(rows, KEY_VALUE_HEADS * HEAD_SIZE)
    gain_attn = (
        jnp.sum(raw_q * low_q, axis=1)
        + jnp.sum(raw_k * low_k, axis=1)
        + jnp.sum(raw_v * low_v, axis=1)
    )
    d_input = d_middle + inverse1 * (e1 - hat1 * jnp.mean(e1 * hat1, axis=-1, keepdims=True))
    return (
        output,
        d_input.astype(low)[None],
        raw_q * gain_a,
        raw_k * gain_a,
        raw_v * gain_a,
        out_sum,
        gate_sum,
        up_sum,
        down_sum,
        gain_attn,
        gain_mlp,
    )


def solution(mesh):
    local = head_local if (mesh.shape["dp"], mesh.shape["ctx"]) == (4, 2 * N_Z) else gathered_local
    in_specs = (
        P("dp", "ctx", None),
        P("dp", "ctx", None),
        P("dp"),
        P(("dp", "ctx"), None),
        P(("dp", "ctx"), None),
        P(("dp", "ctx"), None),
        P(("dp", "ctx"), None),
        P(("dp", "ctx"), None),
        P(("dp", "ctx"), None),
        P(("dp", "ctx"), None),
        P(("dp", "ctx")),
        P(("dp", "ctx")),
    )
    out_specs = (
        P("dp", "ctx", None),
        P("dp", "ctx", None),
        P(("dp", "ctx"), None),
        P(("dp", "ctx"), None),
        P(("dp", "ctx"), None),
        P(("dp", "ctx"), None),
        P(("dp", "ctx"), None),
        P(("dp", "ctx"), None),
        P(("dp", "ctx"), None),
        P(("dp", "ctx")),
        P(("dp", "ctx")),
    )
    return jax.shard_map(local, mesh=mesh, in_specs=in_specs, out_specs=out_specs, check_vma=False)
```

```python
import jax
import jax.numpy as jnp
from jax import lax
from jax.experimental import pallas as pl
from jax.experimental.pallas import tpu as pltpu
from jax.sharding import PartitionSpec as P

FF = 8192
QUERY_HEADS = 8
KEY_VALUE_HEADS = 4
HEAD_SIZE = 256


NORM_EPSILON = 1e-06
THETA = 1000042.0


def rope_angles(token_positions, width):
    half_width = width // 2
    frequency = jnp.power(THETA, -(2.0 * jnp.arange(half_width, dtype=jnp.float32) / width))
    angles = token_positions.astype(jnp.float32)[:, None] * frequency[None, :]
    return (jnp.cos(angles)[:, None, :], jnp.sin(angles)[:, None, :])


def apply_rotary(vector, cosine_table, sines_lookup):
    half_width = vector.shape[-1] // 2
    first_half = vector[..., :half_width]
    second_half = vector[..., half_width:]
    return jnp.concatenate(
        [
            first_half * cosine_table - second_half * sines_lookup,
            second_half * cosine_table + first_half * sines_lookup,
        ],
        axis=-1,
    )


def reverse_rotary(vector, cosine_table, sines_lookup):
    half_width = vector.shape[-1] // 2
    first_half = vector[..., :half_width]
    second_half = vector[..., half_width:]
    return jnp.concatenate(
        [
            first_half * cosine_table + second_half * sines_lookup,
            second_half * cosine_table - first_half * sines_lookup,
        ],
        axis=-1,
    )


def norm_backward(d_normed, hat_values, gain_row, inverse):
    scaled = d_normed * gain_row
    return inverse * (scaled - hat_values * jnp.mean(scaled * hat_values, axis=-1, keepdims=True))


def column_product(left, right):
    return jnp.einsum("bd,bf->df", left, right, preferred_element_type=jnp.float32)


def gathered_local(
    layer_input,
    cotangent,
    prefix,
    w_query,
    key_weight,
    value_weight,
    w_out,
    w_gate,
    w_up,
    w_down,
    attention_norm_gain,
    feedforward_norm_gain,
):
    narrow_number_type = jnp.bfloat16
    wide_number_type = jnp.float32
    token_rows = layer_input.shape[1]
    query_group_width = QUERY_HEADS // KEY_VALUE_HEADS
    attention_score_scale = HEAD_SIZE ** (-0.5)
    input_rows_all = layer_input[0].astype(wide_number_type)
    first_row = lax.axis_index("ctx") * token_rows
    token_positions = first_row + jnp.arange(token_rows, dtype=jnp.int32)
    prefix_len = prefix[0]
    cosine_table, sines_lookup = rope_angles(token_positions, HEAD_SIZE)
    attn_kept = (
        lax.all_gather(w_query.astype(narrow_number_type), ("dp", "ctx"), axis=0, tiled=True),
        lax.all_gather(key_weight.astype(narrow_number_type), ("dp", "ctx"), axis=0, tiled=True),
        lax.all_gather(value_weight.astype(narrow_number_type), ("dp", "ctx"), axis=0, tiled=True),
        lax.all_gather(w_out.astype(narrow_number_type), ("dp", "ctx"), axis=0, tiled=True),
        lax.all_gather(
            attention_norm_gain.astype(narrow_number_type), ("dp", "ctx"), axis=0, tiled=True
        ),
    )
    query_w, key_matrix, value_w, out_w, attention_gain = attn_kept
    first_inverse_norm = lax.rsqrt(
        jnp.mean(input_rows_all * input_rows_all, axis=-1, keepdims=True) + NORM_EPSILON
    )
    first_standardized = input_rows_all * first_inverse_norm
    first_normalized = (first_standardized * attention_gain.astype(wide_number_type)).astype(
        narrow_number_type
    )
    query_rows = jnp.dot(
        first_normalized, query_w, preferred_element_type=wide_number_type
    ).reshape(token_rows, QUERY_HEADS, HEAD_SIZE)
    projected_keys = jnp.dot(
        first_normalized, key_matrix, preferred_element_type=wide_number_type
    ).reshape(token_rows, KEY_VALUE_HEADS, HEAD_SIZE)
    value_rows = jnp.dot(first_normalized, value_w, preferred_element_type=wide_number_type).astype(
        narrow_number_type
    )
    rotated_queries = apply_rotary(query_rows, cosine_table, sines_lookup).astype(
        narrow_number_type
    )
    rotated_keys = (
        apply_rotary(projected_keys, cosine_table, sines_lookup)
        .astype(narrow_number_type)
        .reshape(token_rows, KEY_VALUE_HEADS * HEAD_SIZE)
    )
    grouped_queries = rotated_queries.reshape(
        token_rows, KEY_VALUE_HEADS, query_group_width, HEAD_SIZE
    )

    def masked_scores(key_segment, start_row):
        segment_rows = key_segment.shape[0]
        columns = start_row + jnp.arange(segment_rows, dtype=jnp.int32)
        allowed = (columns[None, :] <= token_positions[:, None]) | (columns[None, :] < prefix_len)
        scores = (
            jnp.einsum(
                "bkgd,jkd->kgbj",
                grouped_queries,
                key_segment.reshape(segment_rows, KEY_VALUE_HEADS, HEAD_SIZE),
                preferred_element_type=wide_number_type,
            )
            * attention_score_scale
        )
        return jnp.where(allowed[None, None], scores, -jnp.inf)

    row_maximum = jnp.full(
        (KEY_VALUE_HEADS, query_group_width, token_rows), -1e30, wide_number_type
    )
    key_segment = lax.all_gather(rotated_keys, "ctx", axis=0, tiled=True)
    value_segment = lax.all_gather(value_rows, "ctx", axis=0, tiled=True)
    segment_rows = value_segment.shape[0]
    scores = masked_scores(key_segment, jnp.int32(0))
    new_peak = jnp.maximum(row_maximum, jnp.max(scores, axis=-1))
    soft_part = jnp.exp(scores - new_peak[..., None])
    row_denominator = jnp.sum(soft_part, axis=-1)
    weighted_values = jnp.einsum(
        "kgbj,jkd->bkgd",
        soft_part.astype(narrow_number_type),
        value_segment.reshape(segment_rows, KEY_VALUE_HEADS, HEAD_SIZE),
        preferred_element_type=wide_number_type,
    )
    row_maximum, row_denominator, weighted_values = (new_peak, row_denominator, weighted_values)
    log_total = row_maximum + jnp.log(row_denominator)
    attention_result = weighted_values / jnp.transpose(row_denominator, (2, 0, 1))[..., None]
    attn_out = attention_result.reshape(token_rows, QUERY_HEADS * HEAD_SIZE).astype(
        narrow_number_type
    )
    hidden_middle = input_rows_all + jnp.dot(
        attn_out, out_w, preferred_element_type=wide_number_type
    )
    mlp_kept = (
        lax.all_gather(w_gate.astype(narrow_number_type), ("dp", "ctx"), axis=0, tiled=True),
        lax.all_gather(w_up.astype(narrow_number_type), ("dp", "ctx"), axis=0, tiled=True),
        lax.all_gather(w_down.astype(narrow_number_type), ("dp", "ctx"), axis=0, tiled=True),
        lax.all_gather(
            feedforward_norm_gain.astype(narrow_number_type), ("dp", "ctx"), axis=0, tiled=True
        ),
    )
    gate_w, up_w, down_w, feedforward_gain = mlp_kept
    second_inverse_norm = lax.rsqrt(
        jnp.mean(hidden_middle * hidden_middle, axis=-1, keepdims=True) + NORM_EPSILON
    )
    second_standardized = hidden_middle * second_inverse_norm
    second_normalized = (second_standardized * feedforward_gain.astype(wide_number_type)).astype(
        narrow_number_type
    )
    gate_proj = jnp.dot(second_normalized, gate_w, preferred_element_type=wide_number_type)
    up_proj = jnp.dot(second_normalized, up_w, preferred_element_type=wide_number_type)
    hidden = (jax.nn.silu(gate_proj) * up_proj).astype(narrow_number_type)
    result = hidden_middle + jnp.dot(hidden, down_w, preferred_element_type=wide_number_type)
    output = result.astype(narrow_number_type)[None]
    gate_w, up_w, down_w, feedforward_gain = (
        lax.all_gather(w_gate.astype(narrow_number_type), ("dp", "ctx"), axis=0, tiled=True),
        lax.all_gather(w_up.astype(narrow_number_type), ("dp", "ctx"), axis=0, tiled=True),
        lax.all_gather(w_down.astype(narrow_number_type), ("dp", "ctx"), axis=0, tiled=True),
        lax.all_gather(
            feedforward_norm_gain.astype(narrow_number_type), ("dp", "ctx"), axis=0, tiled=True
        ),
    )
    d_out = cotangent[0]
    down_sum = lax.psum_scatter(
        column_product(hidden, d_out), ("dp", "ctx"), scatter_dimension=0, tiled=True
    )
    d_hidden = jnp.einsum("bd,fd->bf", d_out, down_w, preferred_element_type=wide_number_type)
    sigmoid_gate = jax.nn.sigmoid(gate_proj)
    d_gate = (d_hidden * up_proj * sigmoid_gate * (1.0 + gate_proj * (1.0 - sigmoid_gate))).astype(
        narrow_number_type
    )
    d_up = (d_hidden * gate_proj * sigmoid_gate).astype(narrow_number_type)
    second_normalized_gradient = jnp.einsum(
        "bf,df->bd", d_gate, gate_w, preferred_element_type=wide_number_type
    ) + jnp.einsum("bf,df->bd", d_up, up_w, preferred_element_type=wide_number_type)
    gate_and_up = jnp.concatenate([d_gate, d_up], axis=1)
    both_sum = lax.psum_scatter(
        column_product(second_normalized, gate_and_up),
        ("dp", "ctx"),
        scatter_dimension=0,
        tiled=True,
    )
    gate_sum = both_sum[:, :FF]
    up_sum = both_sum[:, FF:]
    feedforward_gain_part = jnp.sum(second_normalized_gradient * second_standardized, axis=0)
    middle_gradient = d_out.astype(wide_number_type) + norm_backward(
        second_normalized_gradient,
        second_standardized,
        feedforward_gain.astype(wide_number_type),
        second_inverse_norm,
    )
    query_w, key_matrix, value_w, out_w, attention_gain = (
        lax.all_gather(w_query.astype(narrow_number_type), ("dp", "ctx"), axis=0, tiled=True),
        lax.all_gather(key_weight.astype(narrow_number_type), ("dp", "ctx"), axis=0, tiled=True),
        lax.all_gather(value_weight.astype(narrow_number_type), ("dp", "ctx"), axis=0, tiled=True),
        lax.all_gather(w_out.astype(narrow_number_type), ("dp", "ctx"), axis=0, tiled=True),
        lax.all_gather(
            attention_norm_gain.astype(narrow_number_type), ("dp", "ctx"), axis=0, tiled=True
        ),
    )
    d_branch = middle_gradient.astype(narrow_number_type)
    out_sum = lax.psum_scatter(
        column_product(attn_out, d_branch), ("dp", "ctx"), scatter_dimension=0, tiled=True
    )
    attention_gradient = jnp.einsum(
        "bd,hd->bh", d_branch, out_w, preferred_element_type=wide_number_type
    ).astype(narrow_number_type)
    attention_group_gradient = attention_gradient.reshape(
        token_rows, KEY_VALUE_HEADS, query_group_width, HEAD_SIZE
    )
    delta_rows = jnp.transpose(
        jnp.sum(attention_group_gradient.astype(wide_number_type) * attention_result, axis=-1),
        (1, 2, 0),
    )
    gathered_keys, gathered_values = (
        lax.all_gather(rotated_keys, "ctx", axis=0, tiled=True),
        lax.all_gather(value_rows, "ctx", axis=0, tiled=True),
    )
    count_of_blocks = gathered_keys.shape[0] // token_rows
    stacked_key_blocks = gathered_keys.reshape(
        count_of_blocks, token_rows, KEY_VALUE_HEADS * HEAD_SIZE
    )
    stacked_value_blocks = gathered_values.reshape(
        count_of_blocks, token_rows, KEY_VALUE_HEADS, HEAD_SIZE
    )

    def back_step(d_query_sum, block_item):
        current_key_block, value_block, block_index = block_item
        scores = masked_scores(current_key_block, block_index * token_rows)
        soft_part = jnp.exp(scores - log_total[..., None])
        d_value_block = jnp.einsum(
            "kgbj,bkgd->jkd",
            soft_part.astype(narrow_number_type),
            attention_group_gradient,
            preferred_element_type=wide_number_type,
        )
        d_probs = jnp.einsum(
            "bkgd,jkd->kgbj",
            attention_group_gradient,
            value_block,
            preferred_element_type=wide_number_type,
        )
        d_scores = (soft_part * (d_probs - delta_rows[..., None])).astype(narrow_number_type)
        key_tensor_triple = current_key_block.reshape(token_rows, KEY_VALUE_HEADS, HEAD_SIZE)
        d_query_sum = d_query_sum + jnp.einsum(
            "kgbj,jkd->bkgd", d_scores, key_tensor_triple, preferred_element_type=wide_number_type
        )
        d_key_block = jnp.einsum(
            "kgbj,bkgd->jkd", d_scores, grouped_queries, preferred_element_type=wide_number_type
        )
        return (d_query_sum, (d_key_block, d_value_block))

    d_query_sum, (key_gradients, value_gradients) = lax.scan(
        back_step,
        jnp.zeros((token_rows, KEY_VALUE_HEADS, query_group_width, HEAD_SIZE), wide_number_type),
        (stacked_key_blocks, stacked_value_blocks, jnp.arange(count_of_blocks, dtype=jnp.int32)),
    )
    key_gradients = (
        key_gradients.reshape(count_of_blocks * token_rows, KEY_VALUE_HEADS * HEAD_SIZE)
        * attention_score_scale
    )
    value_gradients = value_gradients.reshape(
        count_of_blocks * token_rows, KEY_VALUE_HEADS * HEAD_SIZE
    )
    local_keys, own_values = (
        lax.psum_scatter(
            key_gradients.astype(jnp.bfloat16), "ctx", scatter_dimension=0, tiled=True
        ).astype(jnp.float32),
        lax.psum_scatter(
            value_gradients.astype(jnp.bfloat16), "ctx", scatter_dimension=0, tiled=True
        ).astype(jnp.float32),
    )
    d_key = (
        reverse_rotary(
            local_keys.reshape(token_rows, KEY_VALUE_HEADS, HEAD_SIZE), cosine_table, sines_lookup
        )
        .reshape(token_rows, KEY_VALUE_HEADS * HEAD_SIZE)
        .astype(narrow_number_type)
    )
    d_value = own_values.astype(narrow_number_type)
    d_query = reverse_rotary(
        (d_query_sum * attention_score_scale).reshape(token_rows, QUERY_HEADS, HEAD_SIZE),
        cosine_table,
        sines_lookup,
    )
    d_query = d_query.reshape(token_rows, QUERY_HEADS * HEAD_SIZE).astype(narrow_number_type)
    d_projected = jnp.concatenate([d_query, d_key, d_value], axis=1)
    projection_total = lax.psum_scatter(
        column_product(first_normalized, d_projected),
        ("dp", "ctx"),
        scatter_dimension=0,
        tiled=True,
    )
    query_sum = projection_total[:, : QUERY_HEADS * HEAD_SIZE]
    key_gradient_sum = projection_total[
        :, QUERY_HEADS * HEAD_SIZE : QUERY_HEADS * HEAD_SIZE + KEY_VALUE_HEADS * HEAD_SIZE
    ]
    value_gradient_sum = projection_total[
        :, QUERY_HEADS * HEAD_SIZE + KEY_VALUE_HEADS * HEAD_SIZE :
    ]
    first_normalized_gradient = (
        jnp.einsum("bh,dh->bd", d_query, query_w, preferred_element_type=wide_number_type)
        + jnp.einsum("bh,dh->bd", d_key, key_matrix, preferred_element_type=wide_number_type)
        + jnp.einsum("bh,dh->bd", d_value, value_w, preferred_element_type=wide_number_type)
    )
    attention_gain_part = jnp.sum(first_normalized_gradient * first_standardized, axis=0)
    gradient_of_input = middle_gradient + norm_backward(
        first_normalized_gradient,
        first_standardized,
        attention_gain.astype(wide_number_type),
        first_inverse_norm,
    )
    attn_gain_sum, mlp_gain_sum = (
        lax.psum_scatter(attention_gain_part, ("dp", "ctx"), scatter_dimension=0, tiled=True),
        lax.psum_scatter(feedforward_gain_part, ("dp", "ctx"), scatter_dimension=0, tiled=True),
    )
    input_grad = gradient_of_input.astype(narrow_number_type)[None]
    return (
        output,
        input_grad,
        query_sum,
        key_gradient_sum,
        value_gradient_sum,
        out_sum,
        gate_sum,
        up_sum,
        down_sum,
        attn_gain_sum,
        mlp_gain_sum,
    )

N_Z = 4


def after(value, *others):
    return lax.optimization_barrier((value,) + others)[0]


def swap_cores(values):
    return lax.ppermute(values, "ctx", [(i, i ^ 1) for i in range(2 * N_Z)])


def gather_ctx(rows):
    return lax.all_gather(rows, "ctx", axis=0, tiled=True)


def scatter_ctx(partial):
    return lax.psum_scatter(partial, "ctx", scatter_dimension=0, tiled=True).astype(jnp.float32)


def hop(values, lowest, highest):
    moves = [(2 * z, 2 * z + 2) for z in range(lowest, highest + 1)]
    moves += [(2 * (N_Z - 1 - z) + 1, 2 * (N_Z - 1 - z) - 1) for z in range(lowest, highest + 1)]
    return lax.ppermute(values, "ctx", moves)


def sum_step(slots, carried, step):
    low, wide = jnp.bfloat16, jnp.float32
    keep = jnp.where(is_even(), slots[step], slots[N_Z - step])
    give = jnp.where(is_even(), slots[N_Z - step], slots[step])
    total = keep.astype(wide) + swap_cores(give).astype(wide)
    if carried is not None:
        total = total + carried.astype(wide)
    return hop(total.astype(low), 0, N_Z - 1 - step)


def sum_end(slots, carried):
    low, wide = jnp.bfloat16, jnp.float32
    total = slots[0].astype(wide) + carried.astype(wide)
    half = total.shape[0] // 2
    give = jnp.where(is_even(), total[half:], total[:half]).astype(low)
    return jnp.where(is_even(), total[:half], total[half:]) + swap_cores(give).astype(wide)


def send_dp(values, first, second):
    moves = [(d, c, d ^ (second if c % 2 else first)) for d in range(4) for c in range(2 * N_Z)]
    moves = [(d * 2 * N_Z + c, to * 2 * N_Z + c) for d, c, to in moves]
    return lax.ppermute(values, ("dp", "ctx"), moves)


def is_even():
    return lax.axis_index("ctx") % 2 == 0


def near_bit():
    return jnp.where(is_even(), 1, 2)


def place_dp(rows, first, second, third):
    d = lax.axis_index("dp")
    size = rows.shape[0]
    whole = jnp.zeros((4 * size,) + rows.shape[1:], rows.dtype)
    for block, place in (
        (rows, d),
        (first, d ^ near_bit()),
        (second, d ^ (3 - near_bit())),
        (third, d ^ 3),
    ):
        whole = lax.dynamic_update_slice_in_dim(whole, block, place * size, 0)
    return whole


def stack_dp(rows, first, second, third):
    one = jnp.where(is_even(), first, second)
    two = jnp.where(is_even(), second, first)
    return jnp.concatenate([rows, one, two, third], axis=0)


def exchange_ctx(blocks):
    return lax.all_to_all(blocks, "ctx", 0, 0, tiled=True)


def finish_feedforward(sums, w_gate, w_up, gain):
    n_ctx, rows, both = sums.shape
    part = both // 8

    def kernel(sums_ref, gate_ref, up_ref, gain_ref, gate_out, up_out, gain_out):
        scale = gain_ref[...]
        total = jnp.zeros((rows, part), jnp.float32)
        for d in range(4):
            for c in range(n_ctx):
                place = pl.ds((d * n_ctx + c) * part, part)
                for half, weight_ref, out_ref in ((0, gate_ref, gate_out), (1, up_ref, up_out)):
                    raw = sums_ref[c, :, pl.ds((half * 4 + d) * part, part)].astype(jnp.float32)
                    weight = weight_ref[:, place].astype(jnp.bfloat16).astype(jnp.float32)
                    total = total + raw * weight
                    out_ref[:, place] = raw * scale
        gain_out[...] = jnp.sum(total, axis=1, keepdims=True)

    return pl.pallas_call(
        kernel,
        out_shape=(
            jax.ShapeDtypeStruct(w_gate.shape, jnp.float32),
            jax.ShapeDtypeStruct(w_up.shape, jnp.float32),
            jax.ShapeDtypeStruct((rows, 1), jnp.float32),
        ),
        compiler_params=pltpu.CompilerParams(vmem_limit_bytes=32 * 1024 * 1024),
        cost_estimate=pl.CostEstimate(
            flops=4 * w_gate.size, bytes_accessed=20 * w_gate.size, transcendentals=0
        ),
    )(sums, w_gate, w_up, gain)


def feedforward(hat, weight, d_hidden):
    rows, depth = hat.shape
    width = weight.shape[1] // 2
    tile, chunk = 256, 256
    tiles = width // tile

    def kernel(hat_ref, gate_ref, up_ref, grad_ref, hidden_ref, out_ref):
        place = pl.multiple_of(pl.program_id(0) * tile, tile)
        for start in range(0, rows, chunk):
            part = pl.ds(start, chunk)
            left = hat_ref[part, :]
            gate = jnp.dot(left, gate_ref[...], preferred_element_type=jnp.float32)
            up = jnp.dot(left, up_ref[...], preferred_element_type=jnp.float32)
            sig = jax.nn.sigmoid(gate)
            silu = gate * sig
            grad = grad_ref[part, :]
            hidden_ref[part, :] = (silu * up).astype(jnp.bfloat16)
            d_gate = grad * up * sig * (1.0 + gate * (1.0 - sig))
            out_ref[part, pl.ds(place, tile)] = d_gate.astype(jnp.bfloat16)
            out_ref[part, pl.ds(width + place, tile)] = (grad * silu).astype(jnp.bfloat16)

    return pl.pallas_call(
        kernel,
        grid=(tiles,),
        in_specs=[
            pl.BlockSpec((rows, depth), lambda j: (0, 0)),
            pl.BlockSpec((depth, tile), lambda j: (0, j)),
            pl.BlockSpec((depth, tile), lambda j: (0, tiles + j)),
            pl.BlockSpec((rows, tile), lambda j: (0, j)),
        ],
        out_specs=(
            pl.BlockSpec((rows, tile), lambda j: (0, j)),
            pl.BlockSpec((rows, 2 * width), lambda j: (0, 0)),
        ),
        out_shape=(
            jax.ShapeDtypeStruct((rows, width), jnp.bfloat16),
            jax.ShapeDtypeStruct((rows, 2 * width), jnp.bfloat16),
        ),
        compiler_params=pltpu.CompilerParams(vmem_limit_bytes=44 * 1024 * 1024),
        cost_estimate=pl.CostEstimate(
            flops=4 * rows * depth * width,
            bytes_accessed=2 * rows * depth + 4 * depth * width + 10 * rows * width,
            transcendentals=rows * width,
        ),
    )(hat, weight, weight, d_hidden)


def out_weight_moves():
    moves = []
    for block in range(8 * N_Z):
        head, part = divmod(block, N_Z)
        moves.append((block, part * 2 * N_Z + head))
    return moves


def head_local(
    layer_input,
    cotangent,
    prefix,
    w_query,
    key_weight,
    value_weight,
    w_out,
    w_gate,
    w_up,
    w_down,
    attention_norm_gain,
    feedforward_norm_gain,
):
    low = jnp.bfloat16
    wide = jnp.float32
    d = lax.axis_index("dp")
    even = is_even()
    rows = w_query.shape[0]
    seq_rows = layer_input.shape[1] * 2 * N_Z
    ff_part = w_down.shape[0]
    width = 4 * ff_part
    cols = 2 * HEAD_SIZE

    def dot(left, right):
        return jnp.dot(left, right, preferred_element_type=wide)

    def dot_t(left, right):
        return lax.dot_general(left, right, (((1,), (1,)), ((), ())), preferred_element_type=wide)

    def t_dot(left, right):
        return lax.dot_general(left, right, (((0,), (0,)), ((), ())), preferred_element_type=wide)

    def lowered(weight):
        return weight.astype(low).astype(wide)

    def turned(values):
        size = values.shape[1] // 4
        return jnp.concatenate(
            [lax.dynamic_slice_in_dim(values, (d ^ e) * size, size, 1) for e in range(4)], axis=1
        )

    def block_columns(values, e):
        size = values.shape[1] // 4
        return lax.dynamic_slice_in_dim(values, e * size, size, 1)

    x_rows = layer_input[0].astype(wide)
    d_out = cotangent[0]
    gain_a = lowered(attention_norm_gain)[:, None]
    gain_m = lowered(feedforward_norm_gain)[:, None]
    low_q, low_k, low_v = lowered(w_query), lowered(key_weight), lowered(value_weight)
    low_g, low_u = lowered(w_gate), lowered(w_up)

    moves = out_weight_moves()
    out_own = lax.ppermute(w_out.astype(low), ("dp", "ctx"), moves)

    inverse1 = lax.rsqrt(jnp.mean(x_rows * x_rows, axis=-1, keepdims=True) + NORM_EPSILON)
    hat1 = x_rows * inverse1
    sent1 = turned(layer_input[0])

    q_cols = (low_q * gain_a).astype(low).reshape(rows, N_Z, 2, HEAD_SIZE).transpose(1, 2, 0, 3)
    k_cols = (low_k * gain_a).astype(low).reshape(rows, N_Z, 1, HEAD_SIZE).transpose(1, 2, 0, 3)
    v_cols = (low_v * gain_a).astype(low).reshape(rows, N_Z, 1, HEAD_SIZE).transpose(1, 2, 0, 3)
    proj_blocks = jnp.concatenate([q_cols, jnp.concatenate([k_cols, v_cols], axis=1)], axis=3)
    proj_own = exchange_ctx(proj_blocks.reshape(2 * N_Z, rows, cols))
    all_rows = gather_ctx(sent1)
    proj_own = proj_own.reshape(2 * N_Z * rows, cols)
    proj_first, proj_second = send_dp(proj_own, 1, 2), send_dp(proj_own, 2, 1)
    gain_late = after(gain_m, proj_own)

    def ff_columns(weight):
        blocks = (weight * gain_late).astype(low).reshape(rows, 4, N_Z, 2, ff_part)
        return blocks.transpose(2, 3, 0, 1, 4).reshape(N_Z, 2, rows, width)

    gate_up_blocks = jnp.concatenate([ff_columns(low_g), ff_columns(low_u)], axis=3)
    down_own = w_down.astype(low)
    all_rows, out_own, down_own, gate_up_blocks, proj_first, proj_second = (
        lax.optimization_barrier(
            (all_rows, out_own, down_own, gate_up_blocks, proj_first, proj_second)
        )
    )
    proj_third = send_dp(proj_first, 2, 1)
    all_cot = gather_ctx(after(d_out, all_rows))
    all_rows = all_rows.astype(wide)
    all_hat1 = all_rows * lax.rsqrt(
        jnp.mean(all_rows * all_rows, axis=-1, keepdims=True) + NORM_EPSILON
    )
    all_hat1 = all_hat1.astype(low)
    proj = stack_dp(proj_own, proj_first, proj_second, proj_third)
    gate_up_own = exchange_ctx(gate_up_blocks.reshape(2 * N_Z, rows, 2 * width))
    positions = jnp.arange(seq_rows, dtype=jnp.int32)
    cosine, sine = rope_angles(positions, HEAD_SIZE)
    cosine, sine = cosine[:, 0], sine[:, 0]
    half = HEAD_SIZE // 2

    def rotate(v, turn):
        a, b = v[:, :half], v[:, half:]
        return jnp.concatenate([a * cosine - turn * b * sine, b * cosine + turn * a * sine], axis=1)

    qkv = dot(all_hat1, proj)
    scale = HEAD_SIZE ** (-0.5)
    q_rot = (rotate(qkv[:, :HEAD_SIZE], 1.0) * scale).astype(low)
    own = qkv[:, HEAD_SIZE:]
    own = jnp.where(even, rotate(own, 1.0), own).astype(low)
    own, q_rot, out_own, down_own = lax.optimization_barrier((own, q_rot, out_own, down_own))
    out_first, out_second = send_dp(out_own, 1, 2), send_dp(out_own, 2, 1)
    out_w = place_dp(out_own, out_first, out_second, send_dp(out_first, 2, 1))
    down_first, down_second = send_dp(down_own, 1, 2), send_dp(down_own, 2, 1)
    other = swap_cores(own)
    keys = jnp.where(even, own, other)
    values = jnp.where(even, other, own)
    allowed = (positions[None, :] <= positions[:, None]) | (positions[None, :] < prefix[0])
    scores = jnp.where(allowed, dot_t(q_rot, keys), -1e30)
    peak = jnp.max(scores, axis=-1, keepdims=True)
    weights = jnp.exp(scores - peak)
    total = jnp.sum(weights, axis=-1, keepdims=True)
    attended = dot(weights.astype(low), values) / total
    attn = attended.astype(low)
    branch_part = dot(attn, out_w).astype(low)
    down_third = send_dp(down_first, 2, 1)
    branch_part, all_cot, down_second, down_third, gate_up_own = lax.optimization_barrier(
        (branch_part, all_cot, down_second, down_third, gate_up_own)
    )
    gate_up_own = gate_up_own.reshape(2 * N_Z * rows, 2 * width)
    branch = scatter_ctx(branch_part)
    gu_first, gu_second = send_dp(gate_up_own, 1, 2), send_dp(gate_up_own, 2, 1)
    middle = x_rows + branch

    inverse2 = lax.rsqrt(jnp.mean(middle * middle, axis=-1, keepdims=True) + NORM_EPSILON)
    hat2 = middle * inverse2
    sent2, gu_first, gu_second = lax.optimization_barrier(
        (turned(hat2).astype(low), gu_first, gu_second)
    )
    all_hat2 = gather_ctx(sent2)
    gu_third = send_dp(gu_first, 2, 1)
    gate_up_w = stack_dp(gate_up_own, gu_first, gu_second, gu_third)
    down_w = place_dp(down_own, down_first, down_second, down_third)
    d_hidden = dot_t(all_cot, down_w)
    all_hat2, gate_up_w, down_w, all_cot, d_hidden = lax.optimization_barrier(
        (all_hat2, gate_up_w, down_w, all_cot, d_hidden)
    )
    hidden, d_gate_up = feedforward(all_hat2, gate_up_w, d_hidden)
    e2_part = dot_t(d_gate_up, gate_up_w).astype(low)
    e2 = scatter_ctx(e2_part)
    d_gate_up, hidden = lax.optimization_barrier((d_gate_up, hidden, e2_part))[:2]

    def gu_block(j):
        return t_dot(block_columns(all_hat2, j), d_gate_up)

    def down_block(j):
        return t_dot(block_columns(hidden, d ^ j), all_cot)

    gu_across = send_dp(gu_block(3).astype(low), 2, 1)
    gu_far = send_dp(gu_block(3 - near_bit()).astype(low), 2, 1)
    gu_near_term, gu_own_term = gu_block(near_bit()), gu_block(0)
    z = lax.axis_index("ctx") // 2
    size = seq_rows // N_Z
    out_slots = [
        dot(lax.dynamic_slice_in_dim(hidden, (z + j) % N_Z * size, size, 0), down_w).astype(low)
        for j in range(N_Z)
    ]
    carried = sum_step(out_slots, None, 3)
    down_sent3 = down_block(3).astype(low)
    down_sent_far = down_block(3 - near_bit()).astype(low)
    gu_relay = (gu_near_term + gu_across.astype(wide)).astype(low)
    e2, gu_relay, gu_far, down_sent3, down_sent_far, carried = lax.optimization_barrier(
        (e2, gu_relay, gu_far, down_sent3, down_sent_far, carried)
    )
    gu_near = send_dp(gu_relay, 1, 2)
    gu_own_sum = gu_own_term + gu_far.astype(wide)
    down_across, down_far = send_dp(down_sent3, 2, 1), send_dp(down_sent_far, 2, 1)
    e2 = turned(e2)
    d_middle = d_out.astype(wide) + inverse2 * (
        e2 - hat2 * jnp.mean(e2 * hat2, axis=-1, keepdims=True)
    )
    branch_low = d_middle.astype(low)
    all_branch = gather_ctx(branch_low)
    carried = sum_step(out_slots, carried, 2)
    gate_up_sum = (gu_own_sum + gu_near.astype(wide)).astype(low)

    gate_up_source = gate_up_sum.reshape(2 * N_Z, rows, 2 * width)
    gate_up_sum = exchange_ctx(gate_up_source)
    down_across, down_far = lax.optimization_barrier((down_across, down_far, gate_up_source))[:2]
    down_relay = (down_block(near_bit()) + down_across.astype(wide)).astype(low)
    down_own_sum = down_block(0) + down_far.astype(wide)
    all_branch, down_relay, down_own_sum = lax.optimization_barrier(
        (all_branch, down_relay, down_own_sum, gate_up_source)
    )[:3]
    down_near = send_dp(down_relay, 1, 2)

    def out_block(j):
        return lax.dynamic_slice_in_dim(head_part, (d ^ j) * rows, rows, 0)

    d_attn = dot_t(all_branch, out_w).astype(low)
    head_part = t_dot(attn, after(all_branch, d_attn))
    out_across = send_dp(out_block(3).astype(low), 2, 1)
    out_far = send_dp(out_block(3 - near_bit()).astype(low), 2, 1)
    delta = jnp.sum(d_attn.astype(wide) * attended, axis=-1, keepdims=True)
    probs = weights / total
    d_scores = (probs * (dot_t(d_attn, values) - delta)).astype(low)
    d_scores, out_across, carried = lax.optimization_barrier((d_scores, out_across, carried))
    out_near = send_dp((out_block(near_bit()) + out_across.astype(wide)).astype(low), 1, 2)
    d_query = rotate(dot(d_scores, keys) * scale, -1.0)
    dk_part = t_dot(d_scores, q_rot)
    dv_part = t_dot(probs.astype(low), d_attn)
    mine = jnp.where(even, dk_part, dv_part)
    mine = mine + swap_cores(jnp.where(even, dv_part, dk_part).astype(low)).astype(wide)
    mine = jnp.where(even, rotate(mine, -1.0), mine)
    d_proj = jnp.concatenate([d_query, mine], axis=1).astype(low)
    e1_part = dot_t(d_proj, proj).astype(low)
    e1_part, out_near, down_near, carried = lax.optimization_barrier(
        (e1_part, out_near, down_near, carried)
    )
    e1 = turned(scatter_ctx(e1_part))
    d_proj = after(d_proj, e1_part)

    def proj_block(j):
        return t_dot(block_columns(all_hat1, j), d_proj)

    proj_across = send_dp(proj_block(3).astype(low), 2, 1)
    proj_far = send_dp(proj_block(3 - near_bit()).astype(low), 2, 1)
    relayed = (proj_block(near_bit()) + proj_across.astype(wide)).astype(low)
    relayed, gate_up_sum = lax.optimization_barrier((relayed, gate_up_sum))
    proj_near = send_dp(relayed, 1, 2)
    proj_sum = proj_block(0) + proj_far.astype(wide) + proj_near.astype(wide)
    proj_source = proj_sum.astype(low).reshape(2 * N_Z, rows, cols)
    proj_sum = exchange_ctx(proj_source)
    gate_up_sum, down_near, out_near, carried = lax.optimization_barrier(
        (gate_up_sum, down_near, out_near, carried, proj_source)
    )[:4]
    carried = sum_step(out_slots, carried, 1)
    out_sum = out_block(0) + out_far.astype(wide) + out_near.astype(wide)
    out_sum = lax.ppermute(
        out_sum.astype(low), ("dp", "ctx"), [(to, start) for start, to in moves]
    )
    out_branch = sum_end(out_slots, carried)
    output = (middle + out_branch).astype(low)[None]
    down_sum = down_own_sum + down_near.astype(wide)
    out_sum, proj_sum = lax.optimization_barrier((out_sum, proj_sum))
    out_sum = out_sum.astype(wide)

    gate_sum, up_sum, gain_mlp = finish_feedforward(gate_up_sum, w_gate, w_up, gain_m)
    gain_mlp = gain_mlp[:, 0]
    proj_sum = proj_sum.astype(wide).transpose(1, 0, 2)
    raw_q = proj_sum[:, :, :HEAD_SIZE].reshape(rows, QUERY_HEADS * HEAD_SIZE)
    kv_sum = proj_sum[:, :, HEAD_SIZE:].reshape(rows, KEY_VALUE_HEADS, 2, HEAD_SIZE)
    raw_k = kv_sum[:, :, 0].reshape(rows, KEY_VALUE_HEADS * HEAD_SIZE)
    raw_v = kv_sum[:, :, 1].reshape(rows, KEY_VALUE_HEADS * HEAD_SIZE)
    gain_attn = (
        jnp.sum(raw_q * low_q, axis=1)
        + jnp.sum(raw_k * low_k, axis=1)
        + jnp.sum(raw_v * low_v, axis=1)
    )
    d_input = d_middle + inverse1 * (e1 - hat1 * jnp.mean(e1 * hat1, axis=-1, keepdims=True))
    return (
        output,
        d_input.astype(low)[None],
        raw_q * gain_a,
        raw_k * gain_a,
        raw_v * gain_a,
        out_sum,
        gate_sum,
        up_sum,
        down_sum,
        gain_attn,
        gain_mlp,
    )


def solution(mesh):
    local = head_local if (mesh.shape["dp"], mesh.shape["ctx"]) == (4, 2 * N_Z) else gathered_local
    in_specs = (
        P("dp", "ctx", None),
        P("dp", "ctx", None),
        P("dp"),
        P(("dp", "ctx"), None),
        P(("dp", "ctx"), None),
        P(("dp", "ctx"), None),
        P(("dp", "ctx"), None),
        P(("dp", "ctx"), None),
        P(("dp", "ctx"), None),
        P(("dp", "ctx"), None),
        P(("dp", "ctx")),
        P(("dp", "ctx")),
    )
    out_specs = (
        P("dp", "ctx", None),
        P("dp", "ctx", None),
        P(("dp", "ctx"), None),
        P(("dp", "ctx"), None),
        P(("dp", "ctx"), None),
        P(("dp", "ctx"), None),
        P(("dp", "ctx"), None),
        P(("dp", "ctx"), None),
        P(("dp", "ctx"), None),
        P(("dp", "ctx")),
        P(("dp", "ctx")),
    )
    return jax.shard_map(local, mesh=mesh, in_specs=in_specs, out_specs=out_specs, check_vma=False)
```
